128 devices in a mesh: depth: 4 (over z_hi, core), lat: 32 (over z_lo, x, y).
Axes of the slice: x: 4, y: 4, z: 4 (z_hi: 2, z_lo: 2; z = z_hi * 2 + z_lo), core: 2. Of those that a mesh axis runs over, the one named last changes fastest.
Arguments:
- source_field: float32 [2, 4, 1024, 1024], P(None, None, 'lat'), may hold values from -9 to 9, as said below
- receiver_field: float32 [2, 4, 1024, 1024], P(None, None, 'lat'), may hold values from -9 to 9, as said below
- zone_index: int32 [16, 1024, 1024], P('depth', 'lat'), may hold values from 0 to 2
- blend_weight: int32 [16, 1024, 1024], P('depth', 'lat'), may hold values from 0 to 16
- ref_velocity: float32 [4], replicated, may hold values from 1500 to 4500
- frequencies: int32 [4], replicated, may hold values from 5 to 40
Outputs:
- migrated_image: float32 [16, 1024, 1024], P('depth', 'lat')
The draws below stay inside these ranges and needn't reach their ends.
Inputs may be any that keep to these rules, and one draw needn't show every extreme that they name: `source_field`: surface wavefields of order one. `receiver_field`: recorded wavefields of order one.
All inputs are finite; a program needn't handle non-finite values.
Results may differ from the reference program's by a relative error of at most 0.0003.
Values sent between devices are 32-bit elements; how exact they have to be, the bound alone decides.
A program may use at most 64 MiB of HBM per device.

```python
import math
import jax
import jax.numpy as jnp
from jax import lax

NY = 1024
NFREQ = 4
NREF = 4
HALF = 7
BLEND = 16
NX = 1024
NZ = 16


def plane_waves(key):
    keys = jax.random.split(key, 5)
    wave_count = 8
    spread = 0.6
    amplitude = jax.random.uniform(keys[0], (NFREQ, wave_count), jnp.float32, -spread, spread)
    along_x = jax.random.uniform(keys[1], (NFREQ, wave_count), jnp.float32, -0.25, 0.25)
    along_y = jax.random.uniform(keys[2], (NFREQ, wave_count), jnp.float32, -0.25, 0.25)
    offset_phase = jax.random.uniform(keys[3], (NFREQ, wave_count), jnp.float32, 0.0, 2.0 * math.pi)
    coord_x = jnp.arange(NX, dtype=jnp.float32)[:, None]
    coord_y = jnp.arange(NY, dtype=jnp.float32)[None, :]
    field_re = jnp.zeros((NFREQ, NX, NY), jnp.float32)
    field_im = jnp.zeros((NFREQ, NX, NY), jnp.float32)
    for number in range(wave_count):
        argument = along_x[:, number, None, None] * coord_x[None] + along_y[:, number, None, None] * coord_y[None] + offset_phase[:, number, None, None]
        field_re = field_re + amplitude[:, number, None, None] * jnp.cos(argument)
        field_im = field_im + amplitude[:, number, None, None] * jnp.sin(argument)
    noise = 0.4 * jax.random.truncated_normal(keys[4], -3.0, 3.0, (2, NFREQ, NX, NY), jnp.float32)
    return jnp.stack([field_re, field_im]) + noise


def draw_source_field(key, part):
    return plane_waves(jax.random.fold_in(key, 11)).astype(jnp.float32)


def draw_receiver_field(key, part):
    return plane_waves(jax.random.fold_in(key, 23)).astype(jnp.float32)


def set_ends(values, own_key, smallest, high):
    place = [jax.random.randint(jax.random.fold_in(own_key, axis), (), 0, length) for axis, length in enumerate(values.shape)]
    main_axis = values.shape.index(max(values.shape))
    next_to = place[:main_axis] + [(place[main_axis] + 1) % values.shape[main_axis]] + place[main_axis + 1:]
    return values.at[tuple(place)].set(smallest).at[tuple(next_to)].set(high)


def setup_inputs(seed: int = 0) -> dict:
    key_of = jax.random.split(jax.random.key(seed), 7)
    return {
        "source_field": draw_source_field(jax.random.fold_in(key_of[6], 71), 0),
        "receiver_field": draw_receiver_field(jax.random.fold_in(key_of[6], 71), 0),
        "zone_index": set_ends(jax.random.randint(key_of[2], (NZ, NX, NY), 0, NREF - 1), jax.random.fold_in(key_of[2], 1), 0, (NREF - 1) - 1).astype(jnp.int32),
        "blend_weight": set_ends(jax.random.randint(key_of[3], (NZ, NX, NY), 0, BLEND + 1), jax.random.fold_in(key_of[3], 1), 0, BLEND).astype(jnp.int32),
        "ref_velocity": jnp.clip(jax.random.uniform(key_of[4], (NREF,), jnp.float32, 1500.0, 4500.0), 1500.0, 4500.0),
        "frequencies": set_ends(jax.random.randint(key_of[5], (NFREQ,), 5, 41), jax.random.fold_in(key_of[5], 1), 5, 40).astype(jnp.int32),
    }


cell_width = 5.0
depth_step = 10.0
taper_width = 16.0

def kernels(frequencies, ref_velocity):
    offsets = jnp.arange(-HALF, HALF + 1, dtype=jnp.int32).astype(jnp.float32)
    wavenumber = 2.0 * math.pi * frequencies.astype(jnp.float32)[:, None] / ref_velocity[None, :]
    curvature = wavenumber * (cell_width * cell_width / (2.0 * depth_step))
    phase_turn = wavenumber * depth_step
    chirp_angle = curvature[:, :, None] * (offsets * offsets)[None, None, :]
    envelope = jnp.exp(-offsets * offsets / taper_width)
    raw_re = envelope * jnp.cos(chirp_angle)
    raw_im = envelope * jnp.sin(chirp_angle)
    magnitude = jnp.sqrt(lax.optimization_barrier(jnp.sum(raw_re, axis=-1)) ** 2 + lax.optimization_barrier(jnp.sum(raw_im, axis=-1)) ** 2)[:, :, None]
    return (raw_re / magnitude, raw_im / magnitude, jnp.cos(phase_turn), jnp.sin(phase_turn))

def convolve_rows(real, imag, tap_re, tap_im):
    length = real.shape[0] - 2 * HALF
    out_re = jnp.zeros((tap_re.shape[0], length, real.shape[1]), jnp.float32)
    out_im = jnp.zeros((tap_re.shape[0], length, real.shape[1]), jnp.float32)
    for offset in range(2 * HALF + 1):
        part_re = real[offset:offset + length][None]
        part_im = imag[offset:offset + length][None]
        coef_re = tap_re[:, offset][:, None, None]
        coef_im = tap_im[:, offset][:, None, None]
        out_re = out_re + coef_re * part_re - coef_im * part_im
        out_im = out_im + coef_re * part_im + coef_im * part_re
    return (out_re, out_im)

def convolve_cols(real, imag, tap_re, tap_im):
    length = real.shape[2] - 2 * HALF
    out_re = jnp.zeros(real.shape[:2] + (length,), jnp.float32)
    out_im = jnp.zeros(real.shape[:2] + (length,), jnp.float32)
    for offset in range(2 * HALF + 1):
        part_re = real[:, :, offset:offset + length]
        part_im = imag[:, :, offset:offset + length]
        coef_re = tap_re[:, offset][:, None, None]
        coef_im = tap_im[:, offset][:, None, None]
        out_re = out_re + coef_re * part_re - coef_im * part_im
        out_im = out_im + coef_re * part_im + coef_im * part_re
    return (out_re, out_im)

def advance(pad_re, pad_im, tap_re, tap_im, turn_cos, turn_sin, zone_level, weight_level):
    rows_re, rows_im = convolve_rows(pad_re, pad_im, tap_re, tap_im)
    widths = ((0, 0), (0, 0), (HALF, HALF))
    both_re, both_im = convolve_cols(jnp.pad(rows_re, widths), jnp.pad(rows_im, widths), tap_re, tap_im)
    phased_re = both_re * turn_cos[:, None, None] - both_im * turn_sin[:, None, None]
    phased_im = both_re * turn_sin[:, None, None] + both_im * turn_cos[:, None, None]
    reference_ids = jnp.arange(tap_re.shape[0], dtype=jnp.int32)[:, None, None]
    weights = jnp.where(reference_ids == zone_level[None], 1.0 - weight_level[None], 0.0)
    weights = weights + jnp.where(reference_ids == zone_level[None] + 1, weight_level[None], 0.0)
    return (lax.optimization_barrier(jnp.sum(weights * phased_re, axis=0)), lax.optimization_barrier(jnp.sum(weights * phased_im, axis=0)))

def reference(source_field, receiver_field, zone_index, blend_weight, ref_velocity, frequencies):
    tap_re, tap_im, turn_cos, turn_sin = kernels(frequencies, ref_velocity)
    weight_levels = blend_weight.astype(jnp.float32) / BLEND
    widths = ((HALF, HALF), (0, 0))

    def each_frequency(migrated, which):

        def each_level(fields, depth_level):
            source_re, source_im, receiver_re, receiver_im = fields
            zone_level = zone_index[depth_level]
            weight_level = weight_levels[depth_level]
            source_re, source_im = advance(jnp.pad(source_re, widths), jnp.pad(source_im, widths), tap_re[which], tap_im[which], turn_cos[which], turn_sin[which], zone_level, weight_level)
            receiver_re, receiver_im = advance(jnp.pad(receiver_re, widths), jnp.pad(receiver_im, widths), tap_re[which], -tap_im[which], turn_cos[which], -turn_sin[which], zone_level, weight_level)
            return ((source_re, source_im, receiver_re, receiver_im), source_re * receiver_re + source_im * receiver_im)
        start = (source_field[0, which], source_field[1, which], receiver_field[0, which], receiver_field[1, which])
        _, pieces = lax.scan(each_level, start, jnp.arange(NZ, dtype=jnp.int32))
        return (migrated + pieces, None)
    migrated, _ = lax.scan(each_frequency, jnp.zeros((NZ, NX, NY), jnp.float32), jnp.arange(NFREQ, dtype=jnp.int32))
    return migrated / NFREQ
```

```python
import functools
import math

import jax
import jax.numpy as jnp
from jax import lax
from jax.experimental import pallas as pl
from jax.experimental.pallas import tpu as pltpu
from jax.sharding import PartitionSpec as P

HALF = 7
BLEND = 16
LANES = 128
PAD = 128
STEP = LANES - 2 * HALF
HALO = 8
GROUP = 16

cell_width = 5.0
depth_step = 10.0
taper_width = 16.0


def kernels(frequency, ref_velocity):
    offsets = jnp.arange(0, HALF + 1, dtype=jnp.int32).astype(jnp.float32)
    wavenumber = 2.0 * math.pi * frequency.astype(jnp.float32) / ref_velocity
    curvature = wavenumber * (cell_width * cell_width / (2.0 * depth_step))
    phase_turn = wavenumber * depth_step
    chirp_angle = curvature[:, None] * (offsets * offsets)[None, :]
    envelope = jnp.exp(-offsets * offsets / taper_width)
    raw_re = envelope * jnp.cos(chirp_angle)
    raw_im = envelope * jnp.sin(chirp_angle)
    both = jnp.where(offsets == 0.0, 1.0, 2.0)
    magnitude = jnp.sqrt(
        jnp.sum(both * raw_re, axis=-1) ** 2 + jnp.sum(both * raw_im, axis=-1) ** 2
    )[:, None]
    return raw_re / magnitude, raw_im / magnitude, jnp.cos(phase_turn), jnp.sin(phase_turn)


def split(x):
    high = lax.reduce_precision(x, 8, 7)
    return high.astype(jnp.bfloat16), (x - high).astype(jnp.bfloat16)


def banded(taps, distance, keep):
    out = jnp.zeros((taps.shape[0],) + distance.shape, jnp.float32)
    for m in range(HALF + 1):
        out = jnp.where((distance == m) & keep, taps[:, m][:, None, None], out)
    return out


def matrices(frequency, ref_velocity):
    c_re, c_im, turn_cos, turn_sin = kernels(frequency, ref_velocity)
    refs = c_re.shape[0]
    r = jnp.arange(GROUP)[:, None]
    k = jnp.arange(2 * GROUP)[None, :]
    distance = jnp.abs(k - HALO - r)
    a_re, a_im = (banded(t, distance, True) for t in (c_re, c_im))
    x_mat = jnp.concatenate(
        [jnp.concatenate([a_re, -a_im], 2), jnp.concatenate([a_im, a_re], 2)], 1
    ).reshape(refs * 2 * GROUP, 4 * GROUP)
    x_high, x_low = split(x_mat)
    x_all = jnp.concatenate([x_high, x_high, x_low], 1)
    d_re = c_re * turn_cos[:, None] - c_im * turn_sin[:, None]
    d_im = c_re * turn_sin[:, None] + c_im * turn_cos[:, None]
    k = jnp.arange(LANES)[:, None]
    n = jnp.arange(LANES)[None, :]
    distance = jnp.abs(k - HALF - n)
    b_re, b_im = (banded(t, distance, n < STEP) for t in (d_re, d_im))
    y_mat = jnp.concatenate(
        [jnp.concatenate([b_re, b_im], 2), jnp.concatenate([-b_im, b_re], 2)], 1
    )
    y_high, y_low = split(y_mat)
    return x_all, jnp.concatenate([y_high, y_high, y_low], 1)


def two_parts(x):
    high = x.astype(jnp.bfloat16)
    return high, (x - high.astype(jnp.float32)).astype(jnp.bfloat16)


def body(
    lat_size, source, receiver, zone, blend, x_mat, y_mat,
    image, field, halo, xbuf, ybuf, load_sem, send_sem, recv_sem,
):
    levels = zone.shape[0]
    rows, cols = zone.shape[1:]
    refs = y_mat.shape[0]
    windows = -(-cols // STEP)
    lat = lax.axis_index("lat")
    chosen = lax.axis_index("depth")
    has_up = lat > 0
    has_down = lat < lat_size - 1
    inner = pl.ds(PAD, cols)

    loads = [
        pltpu.make_async_copy(
            ref.at[:, chosen], field.at[f, :, :, inner], load_sem.at[f]
        )
        for f, ref in enumerate((source, receiver))
    ]
    for load in loads:
        load.start()
    halo[...] = jnp.zeros_like(halo)
    for f in range(2):
        for c in range(2):
            field[f, c, :, 0:PAD] = jnp.zeros((rows, PAD), jnp.float32)
            field[f, c, :, PAD + cols :] = jnp.zeros((rows, PAD), jnp.float32)

    barrier = pltpu.get_barrier_semaphore()

    @pl.when(has_up)
    def _():
        pl.semaphore_signal(barrier, inc=1, device_id={"lat": lat - 1})

    @pl.when(has_down)
    def _():
        pl.semaphore_signal(barrier, inc=1, device_id={"lat": lat + 1})

    pl.semaphore_wait(barrier, has_up.astype(jnp.int32) + has_down.astype(jnp.int32))

    def to_up(f, slot):
        return pltpu.make_async_remote_copy(
            src_ref=field.at[f, :, pl.ds(0, HALO), inner],
            dst_ref=halo.at[slot, f, 1, :, :, inner],
            send_sem=send_sem.at[f, 0],
            recv_sem=recv_sem.at[slot, f, 1],
            device_id={"lat": lat - 1},
        )

    def to_down(f, slot):
        return pltpu.make_async_remote_copy(
            src_ref=field.at[f, :, pl.ds(rows - HALO, HALO), inner],
            dst_ref=halo.at[slot, f, 0, :, :, inner],
            send_sem=send_sem.at[f, 1],
            recv_sem=recv_sem.at[slot, f, 0],
            device_id={"lat": lat + 1},
        )

    def each_side(act_up, act_down):
        @pl.when(has_up)
        def _():
            act_up()

        @pl.when(has_down)
        def _():
            act_down()

    def send(f, slot):
        each_side(lambda: to_up(f, slot).start(), lambda: to_down(f, slot).start())

    def wait_sent(f, slot):
        each_side(lambda: to_up(f, slot).wait_send(), lambda: to_down(f, slot).wait_send())

    def wait_arrived(f, slot):
        each_side(lambda: to_down(f, slot).wait_recv(), lambda: to_up(f, slot).wait_recv())

    for f in range(2):
        loads[f].wait()
        if f == 1:
            field[1, 1] = -field[1, 1]
        send(f, 0)

    def level(z, carry):
        slot = lax.rem(z, 2)
        for f in range(2):
            wait_arrived(f, slot)
            for w in range(windows):
                at = pl.ds(PAD + w * STEP - HALF, LANES)
                parts = []
                for group in range(rows // GROUP):
                    column = []
                    for c in range(2):
                        first = group * GROUP - HALO
                        pieces = []
                        if first < 0:
                            pieces.append(halo[slot, f, 0, c, :, at])
                        low, high = max(first, 0), min(first + 2 * GROUP, rows)
                        pieces.append(field[f, c, low:high, at])
                        if first + 2 * GROUP > rows:
                            pieces.append(halo[slot, f, 1, c, :, at])
                        column.append(jnp.concatenate(pieces, 0))
                    parts.append(jnp.concatenate(column, 0))
                high, low = two_parts(jnp.concatenate(parts, 1))
                out = jnp.dot(
                    x_mat[...],
                    jnp.concatenate([high, low, high], 0),
                    preferred_element_type=jnp.float32,
                )
                for part, values in enumerate(two_parts(out)):
                    for j in range(refs):
                        for c in range(2):
                            for group in range(rows // GROUP):
                                top = (j * 2 + c) * GROUP
                                left = group * LANES
                                xbuf[
                                    j,
                                    w * rows + group * GROUP : w * rows + (group + 1) * GROUP,
                                    (part * 2 + c) * LANES : (part * 2 + c + 1) * LANES,
                                ] = values[top : top + GROUP, left : left + LANES]
            wait_sent(f, slot)
            for j in range(refs):
                ybuf[j] = jnp.dot(
                    jnp.concatenate([xbuf[j], xbuf[j, :, 0 : 2 * LANES]], 1),
                    y_mat[j],
                    preferred_element_type=jnp.float32,
                )
            for w in range(windows):
                width = min(STEP, cols - w * STEP)
                here = pl.ds(w * STEP, width)
                which = zone[z, :, here]
                upper = blend[z, :, here].astype(jnp.float32) * (1.0 / BLEND)
                lower = 1.0 - upper
                total = [jnp.zeros((rows, width), jnp.float32)] * 2
                for j in range(refs):
                    weight = jnp.where(which == j, lower, jnp.where(which == j - 1, upper, 0.0))
                    for c in range(2):
                        total[c] = total[c] + weight * (
                            ybuf[j, w * rows : (w + 1) * rows, c * LANES : c * LANES + width]
                        )
                for c in range(2):
                    field[f, c, :, pl.ds(PAD + w * STEP, width)] = total[c]

            @pl.when(z < levels - 1)
            def _():
                send(f, 1 - slot)

        image[z] = (
            field[0, 0, :, inner] * field[1, 0, :, inner]
            - field[0, 1, :, inner] * field[1, 1, :, inner]
        )
        return carry

    lax.fori_loop(0, levels, level, 0)


def migrate(lat_size, source, receiver, zone, blend, x_mat, y_mat):
    levels, rows, cols = zone.shape
    windows = -(-cols // STEP)
    refs = y_mat.shape[0]
    vmem = pl.BlockSpec(memory_space=pltpu.VMEM)
    hbm = pl.BlockSpec(memory_space=pl.ANY)
    wide = cols + 2 * PAD
    return pl.pallas_call(
        functools.partial(body, lat_size),
        out_shape=jax.ShapeDtypeStruct((levels, rows, cols), jnp.float32),
        in_specs=[hbm, hbm, vmem, vmem, vmem, vmem],
        out_specs=vmem,
        scratch_shapes=[
            pltpu.VMEM((2, 2, rows, wide), jnp.float32),
            pltpu.VMEM((2, 2, 2, 2, HALO, wide), jnp.float32),
            pltpu.VMEM((refs, windows * rows, 4 * LANES), jnp.bfloat16),
            pltpu.VMEM((refs, windows * rows, 2 * LANES), jnp.float32),
            pltpu.SemaphoreType.DMA((2,)),
            pltpu.SemaphoreType.DMA((2, 2)),
            pltpu.SemaphoreType.DMA((2, 2, 2)),
        ],
        compiler_params=pltpu.CompilerParams(
            collective_id=0, has_side_effects=True, vmem_limit_bytes=60 * 2**20
        ),
    )(source, receiver, zone, blend, x_mat, y_mat)


def local(lat_size, source_field, receiver_field, zone_index, blend_weight, ref_velocity, frequencies):
    group_index = lax.axis_index("depth")
    groups = lax.axis_size("depth")
    freq_count = source_field.shape[1]
    frequency = lax.dynamic_index_in_dim(frequencies, group_index, keepdims=False)
    x_mat, y_mat = matrices(frequency, ref_velocity)
    rows = zone_index.shape[1]
    both = lax.all_gather(
        jnp.concatenate([zone_index, blend_weight], axis=1), "depth", axis=0, tiled=True
    )
    pieces = migrate(
        lat_size, source_field, receiver_field, both[:, :rows], both[:, rows:], x_mat, y_mat
    )
    blocks = pieces.reshape(groups, -1, *pieces.shape[1:])
    arrived = lax.all_to_all(blocks, "depth", split_axis=0, concat_axis=0, tiled=True)
    return arrived.sum(axis=0) / freq_count


def solution(mesh):
    in_specs = (
        P(None, None, "lat", None),
        P(None, None, "lat", None),
        P("depth", "lat", None),
        P("depth", "lat", None),
        P(),
        P(),
    )
    out_specs = P("depth", "lat", None)
    return jax.shard_map(
        functools.partial(local, mesh.shape["lat"]),
        mesh=mesh, in_specs=in_specs, out_specs=out_specs, check_vma=False,
    )
```

```python
import functools
import math

import jax
import jax.numpy as jnp
from jax import lax
from jax.experimental import pallas as pl
from jax.experimental.pallas import tpu as pltpu
from jax.sharding import PartitionSpec as P

HALF = 7
BLEND = 16
LANES = 128
PAD = 128
STEP = LANES - 2 * HALF
HALO = 8
GROUP = 16

cell_width = 5.0
depth_step = 10.0
taper_width = 16.0


def kernels(frequency, ref_velocity):
    offsets = jnp.arange(0, HALF + 1, dtype=jnp.int32).astype(jnp.float32)
    wavenumber = 2.0 * math.pi * frequency.astype(jnp.float32) / ref_velocity
    curvature = wavenumber * (cell_width * cell_width / (2.0 * depth_step))
    phase_turn = wavenumber * depth_step
    chirp_angle = curvature[:, None] * (offsets * offsets)[None, :]
    envelope = jnp.exp(-offsets * offsets / taper_width)
    raw_re = envelope * jnp.cos(chirp_angle)
    raw_im = envelope * jnp.sin(chirp_angle)
    both = jnp.where(offsets == 0.0, 1.0, 2.0)
    magnitude = jnp.sqrt(
        jnp.sum(both * raw_re, axis=-1) ** 2 + jnp.sum(both * raw_im, axis=-1) ** 2
    )[:, None]
    return raw_re / magnitude, raw_im / magnitude, jnp.cos(phase_turn), jnp.sin(phase_turn)


def split(x):
    high = lax.reduce_precision(x, 8, 7)
    return high.astype(jnp.bfloat16), (x - high).astype(jnp.bfloat16)


def banded(taps, distance, keep):
    out = jnp.zeros((taps.shape[0],) + distance.shape, jnp.float32)
    for m in range(HALF + 1):
        out = jnp.where((distance == m) & keep, taps[:, m][:, None, None], out)
    return out


def matrices(frequency, ref_velocity):
    c_re, c_im, turn_cos, turn_sin = kernels(frequency, ref_velocity)
    refs = c_re.shape[0]
    r = jnp.arange(GROUP)[:, None]
    k = jnp.arange(2 * GROUP)[None, :]
    distance = jnp.abs(k - HALO - r)
    a_re, a_im = (banded(t, distance, True) for t in (c_re, c_im))
    x_mat = jnp.concatenate(
        [jnp.concatenate([a_re, -a_im], 2), jnp.concatenate([a_im, a_re], 2)], 1
    ).reshape(refs * 2 * GROUP, 4 * GROUP)
    x_high, x_low = split(x_mat)
    x_all = jnp.concatenate([x_high, x_high, x_low], 1)
    d_re = c_re * turn_cos[:, None] - c_im * turn_sin[:, None]
    d_im = c_re * turn_sin[:, None] + c_im * turn_cos[:, None]
    k = jnp.arange(LANES)[:, None]
    n = jnp.arange(LANES)[None, :]
    distance = jnp.abs(k - HALF - n)
    b_re, b_im = (banded(t, distance, n < STEP) for t in (d_re, d_im))
    y_mat = jnp.concatenate(
        [jnp.concatenate([b_re, b_im], 2), jnp.concatenate([-b_im, b_re], 2)], 1
    )
    y_high, y_low = split(y_mat)
    return x_all, jnp.concatenate([y_high, y_high, y_low], 1)


def two_parts(x):
    high = x.astype(jnp.bfloat16)
    return high, (x - high.astype(jnp.float32)).astype(jnp.bfloat16)


def body(
    lat_size, source, receiver, zone, blend, x_mat, y_mat,
    image, field, halo, table, weights, xbuf, ybuf, part, arrived,
    load_sem, table_sem, table_sent, send_sem, recv_sem, part_sem, part_sent,
):
    own_levels, rows, cols = zone.shape
    levels, width_all = table.shape[1], table.shape[3]
    depths = levels // own_levels
    pairs = x_mat.shape[0]
    refs = y_mat.shape[1]
    half = part.shape[2]
    windows = -(-width_all // STEP)
    lat = lax.axis_index("lat")
    me = lax.axis_index("depth")
    side, core = me // 2, lax.rem(me, 2)
    has_up = lat > 0
    has_down = lat < lat_size - 1
    inner = pl.ds(PAD, width_all)

    def columns_of(device):
        return pl.ds(pl.multiple_of((device // 2) * (cols - width_all), LANES), width_all)

    peers = [side * 2 + 1 - core, (1 - side) * 2 + core, (1 - side) * 2 + 1 - core]
    tables = (zone, blend)

    loads = [
        pltpu.make_async_copy(
            ref.at[:, core * pairs + q, :, columns_of(me)],
            field.at[2 * q + f, :, :, inner],
            load_sem.at[2 * q + f],
        )
        for q in range(pairs)
        for f, ref in enumerate((source, receiver))
    ]
    for load in loads:
        load.start()

    def own_table(a, n):
        at = me * own_levels + n
        return pltpu.make_async_copy(
            tables[a].at[n, :, columns_of(me)], table.at[a, at], table_sem.at[a, at]
        )

    def peer_table(i, a, n):
        at = me * own_levels + n
        return pltpu.make_async_remote_copy(
            src_ref=tables[a].at[n, :, columns_of(peers[i])],
            dst_ref=table.at[a, at],
            send_sem=table_sent.at[i, a, n],
            recv_sem=table_sem.at[a, at],
            device_id={"depth": peers[i]},
        )

    every_table = [(i, a, n) for n in range(own_levels) for i in range(3) for a in range(2)]
    for n in range(own_levels):
        for a in range(2):
            own_table(a, n).start()
    halo[...] = jnp.zeros_like(halo)
    for s in range(2 * pairs):
        for c in range(2):
            field[s, c, :, 0:PAD] = jnp.zeros((rows, PAD), jnp.float32)
            field[s, c, :, PAD + width_all :] = jnp.zeros((rows, PAD), jnp.float32)

    barrier = pltpu.get_barrier_semaphore()

    @pl.when(has_up)
    def _():
        pl.semaphore_signal(barrier, inc=1, device_id={"lat": lat - 1})

    @pl.when(has_down)
    def _():
        pl.semaphore_signal(barrier, inc=1, device_id={"lat": lat + 1})

    for peer in peers:
        pl.semaphore_signal(barrier, inc=1, device_id={"depth": peer})
    pl.semaphore_wait(
        barrier, len(peers) + has_up.astype(jnp.int32) + has_down.astype(jnp.int32)
    )

    def to_up(s, slot):
        return pltpu.make_async_remote_copy(
            src_ref=field.at[s, :, pl.ds(0, HALO), inner],
            dst_ref=halo.at[slot, s, 1, :, :, inner],
            send_sem=send_sem.at[s, 0],
            recv_sem=recv_sem.at[slot, s, 1],
            device_id={"lat": lat - 1},
        )

    def to_down(s, slot):
        return pltpu.make_async_remote_copy(
            src_ref=field.at[s, :, pl.ds(rows - HALO, HALO), inner],
            dst_ref=halo.at[slot, s, 0, :, :, inner],
            send_sem=send_sem.at[s, 1],
            recv_sem=recv_sem.at[slot, s, 0],
            device_id={"lat": lat + 1},
        )

    def each_side(act_up, act_down):
        @pl.when(has_up)
        def _():
            act_up()

        @pl.when(has_down)
        def _():
            act_down()

    def send(s, slot):
        each_side(lambda: to_up(s, slot).start(), lambda: to_down(s, slot).start())

    def wait_sent(s, slot):
        each_side(lambda: to_up(s, slot).wait_send(), lambda: to_down(s, slot).wait_send())

    def wait_arrived(s, slot):
        each_side(lambda: to_down(s, slot).wait_recv(), lambda: to_up(s, slot).wait_recv())

    for s in range(2 * pairs):
        loads[s].wait()
        if s % 2 == 1:
            field[s, 1] = -field[s, 1]
        send(s, 0)
    for one in every_table:
        peer_table(*one).start()

    def part_copy(z):
        return pltpu.make_async_remote_copy(
            src_ref=part.at[z],
            dst_ref=arrived.at[lax.rem(z, own_levels), me],
            send_sem=part_sent.at[z],
            recv_sem=part_sem.at[lax.rem(z, own_levels), me],
            device_id={"depth": z // own_levels},
        )

    def level(z, carry):
        slot = lax.rem(z, 2)
        for a in range(2):
            pltpu.make_async_copy(table.at[a, z], table.at[a, z], table_sem.at[a, z]).wait()
        for w in range(windows):
            width = min(STEP, width_all - w * STEP)
            here = pl.ds(w * STEP, width)
            which = table[0, z, :, here]
            upper = table[1, z, :, here].astype(jnp.float32) * (1.0 / BLEND)
            lower = 1.0 - upper
            for j in range(refs):
                weights[j, w * rows : (w + 1) * rows, 0:width] = jnp.where(
                    which == j, lower, jnp.where(which == j - 1, upper, 0.0)
                )
        for s in range(2 * pairs):
            q = s // 2
            wait_arrived(s, slot)
            for w in range(windows):
                at = pl.ds(PAD + w * STEP - HALF, LANES)
                parts = []
                for group in range(rows // GROUP):
                    column = []
                    for c in range(2):
                        first = group * GROUP - HALO
                        pieces = []
                        if first < 0:
                            pieces.append(halo[slot, s, 0, c, :, at])
                        low, high = max(first, 0), min(first + 2 * GROUP, rows)
                        pieces.append(field[s, c, low:high, at])
                        if first + 2 * GROUP > rows:
                            pieces.append(halo[slot, s, 1, c, :, at])
                        column.append(jnp.concatenate(pieces, 0))
                    parts.append(jnp.concatenate(column, 0))
                high, low = two_parts(jnp.concatenate(parts, 1))
                out = jnp.dot(
                    x_mat[q],
                    jnp.concatenate([high, low, high], 0),
                    preferred_element_type=jnp.float32,
                )
                for p, values in enumerate(two_parts(out)):
                    for j in range(refs):
                        for c in range(2):
                            for group in range(rows // GROUP):
                                top = (j * 2 + c) * GROUP
                                left = group * LANES
                                xbuf[
                                    j,
                                    w * rows + group * GROUP : w * rows + (group + 1) * GROUP,
                                    (p * 2 + c) * LANES : (p * 2 + c + 1) * LANES,
                                ] = values[top : top + GROUP, left : left + LANES]
            wait_sent(s, slot)
            for j in range(refs):
                ybuf[j] = jnp.dot(
                    jnp.concatenate([xbuf[j], xbuf[j, :, 0 : 2 * LANES]], 1),
                    y_mat[q, j],
                    preferred_element_type=jnp.float32,
                )
            for w in range(windows):
                width = min(STEP, width_all - w * STEP)
                block = slice(w * rows, (w + 1) * rows)
                for c in range(2):
                    total = weights[0, block, 0:width] * ybuf[0, block, c * LANES : c * LANES + width]
                    for j in range(1, refs):
                        total = total + (
                            weights[j, block, 0:width]
                            * ybuf[j, block, c * LANES : c * LANES + width]
                        )
                    field[s, c, :, pl.ds(PAD + w * STEP, width)] = total

            @pl.when(z < levels - 1)
            def _():
                send(s, 1 - slot)

        mine = pl.ds(pl.multiple_of(PAD + side * (width_all - half), LANES), half)
        total = jnp.zeros((rows, half), jnp.float32)
        for q in range(pairs):
            total = total + field[2 * q, 0, :, mine] * field[2 * q + 1, 0, :, mine]
            total = total - field[2 * q, 1, :, mine] * field[2 * q + 1, 1, :, mine]

        @pl.when(z // own_levels == me)
        def _():
            arrived[lax.rem(z, own_levels), me] = total

        @pl.when(z // own_levels != me)
        def _():
            part[z] = total
            part_copy(z).start()

        return carry

    lax.fori_loop(0, levels, level, 0)

    for one in every_table:
        peer_table(*one).wait_send()

    def sent(z, carry):
        @pl.when(z // own_levels != me)
        def _():
            part_copy(z).wait_send()

        return carry

    lax.fori_loop(0, levels, sent, 0)
    for n in range(own_levels):
        for d in range(depths):
            @pl.when(d != me)
            def _():
                pltpu.make_async_copy(
                    arrived.at[n, d], arrived.at[n, d], part_sem.at[n, d]
                ).wait()

        for h in range(depths // 2):
            image[n, :, h * half : (h + 1) * half] = (
                arrived[n, 2 * h] + arrived[n, 2 * h + 1]
            ) * (1.0 / (2 * pairs))


def migrate(lat_size, depths, source, receiver, zone, blend, x_mat, y_mat):
    own_levels, rows, cols = zone.shape
    levels = depths * own_levels
    pairs, refs = y_mat.shape[:2]
    streams = 2 * pairs
    half = cols // 2
    width = half + -(-HALF * levels // LANES) * LANES
    windows = -(-width // STEP)
    vmem = pl.BlockSpec(memory_space=pltpu.VMEM)
    hbm = pl.BlockSpec(memory_space=pl.ANY)
    wide = width + 2 * PAD
    dma = pltpu.SemaphoreType.DMA
    return pl.pallas_call(
        functools.partial(body, lat_size),
        out_shape=jax.ShapeDtypeStruct((own_levels, rows, cols), jnp.float32),
        in_specs=[hbm, hbm, hbm, hbm, vmem, vmem],
        out_specs=vmem,
        scratch_shapes=[
            pltpu.VMEM((streams, 2, rows, wide), jnp.float32),
            pltpu.VMEM((2, streams, 2, 2, HALO, wide), jnp.float32),
            pltpu.VMEM((2, levels, rows, width), jnp.int32),
            pltpu.VMEM((refs, windows * rows, LANES), jnp.float32),
            pltpu.VMEM((refs, windows * rows, 4 * LANES), jnp.bfloat16),
            pltpu.VMEM((refs, windows * rows, 2 * LANES), jnp.float32),
            pltpu.VMEM((levels, rows, half), jnp.float32),
            pltpu.VMEM((own_levels, depths, rows, half), jnp.float32),
            dma((streams,)),
            dma((2, levels)),
            dma((3, 2, own_levels)),
            dma((streams, 2)),
            dma((2, streams, 2)),
            dma((own_levels, depths)),
            dma((levels,)),
        ],
        compiler_params=pltpu.CompilerParams(
            collective_id=0, has_side_effects=True, vmem_limit_bytes=60 * 2**20
        ),
    )(source, receiver, zone, blend, x_mat, y_mat)


def local(lat_size, source_field, receiver_field, zone_index, blend_weight, ref_velocity, frequencies):
    depths = lax.axis_size("depth")
    pairs = source_field.shape[1] // 2
    core = lax.rem(lax.axis_index("depth"), 2)
    chosen = lax.dynamic_slice_in_dim(frequencies, core * pairs, pairs)
    made = [matrices(chosen[q], ref_velocity) for q in range(pairs)]
    x_mat, y_mat = (jnp.stack(m) for m in zip(*made))
    return migrate(
        lat_size, depths, source_field, receiver_field, zone_index, blend_weight, x_mat, y_mat
    )


def solution(mesh):
    in_specs = (
        P(None, None, "lat", None),
        P(None, None, "lat", None),
        P("depth", "lat", None),
        P("depth", "lat", None),
        P(),
        P(),
    )
    out_specs = P("depth", "lat", None)
    return jax.shard_map(
        functools.partial(local, mesh.shape["lat"]),
        mesh=mesh, in_specs=in_specs, out_specs=out_specs, check_vma=False,
    )
```

```python
import functools
import math

import jax
import jax.numpy as jnp
from jax import lax
from jax.experimental import pallas as pl
from jax.experimental.pallas import tpu as pltpu
from jax.sharding import PartitionSpec as P

HALF = 7
BLEND = 16
LANES = 128
PAD = 128
STEP = LANES - 2 * HALF
HALO = 8
GROUP = 16
AHEAD = 2

cell_width = 5.0
depth_step = 10.0
taper_width = 16.0


def kernels(frequency, ref_velocity):
    offsets = jnp.arange(0, HALF + 1, dtype=jnp.int32).astype(jnp.float32)
    wavenumber = 2.0 * math.pi * frequency.astype(jnp.float32) / ref_velocity
    curvature = wavenumber * (cell_width * cell_width / (2.0 * depth_step))
    phase_turn = wavenumber * depth_step
    chirp_angle = curvature[:, None] * (offsets * offsets)[None, :]
    envelope = jnp.exp(-offsets * offsets / taper_width)
    raw_re = envelope * jnp.cos(chirp_angle)
    raw_im = envelope * jnp.sin(chirp_angle)
    both = jnp.where(offsets == 0.0, 1.0, 2.0)
    magnitude = jnp.sqrt(
        jnp.sum(both * raw_re, axis=-1) ** 2 + jnp.sum(both * raw_im, axis=-1) ** 2
    )[:, None]
    return raw_re / magnitude, raw_im / magnitude, jnp.cos(phase_turn), jnp.sin(phase_turn)


def split(x):
    high = lax.reduce_precision(x, 8, 7)
    return high.astype(jnp.bfloat16), (x - high).astype(jnp.bfloat16)


def banded(taps, distance, keep):
    out = jnp.zeros((taps.shape[0],) + distance.shape, jnp.float32)
    for m in range(HALF + 1):
        out = jnp.where((distance == m) & keep, taps[:, m][:, None, None], out)
    return out


def matrices(frequency, ref_velocity):
    c_re, c_im, turn_cos, turn_sin = kernels(frequency, ref_velocity)
    refs = c_re.shape[0]
    r = jnp.arange(GROUP)[:, None]
    k = jnp.arange(2 * GROUP)[None, :]
    distance = jnp.abs(k - HALO - r)
    a_re, a_im = (banded(t, distance, True) for t in (c_re, c_im))
    x_mat = jnp.concatenate(
        [jnp.concatenate([a_re, -a_im], 2), jnp.concatenate([a_im, a_re], 2)], 1
    ).reshape(refs * 2 * GROUP, 4 * GROUP)
    x_high, x_low = split(x_mat)
    x_all = jnp.concatenate([x_high, x_high, x_low], 1)
    d_re = c_re * turn_cos[:, None] - c_im * turn_sin[:, None]
    d_im = c_re * turn_sin[:, None] + c_im * turn_cos[:, None]
    k = jnp.arange(LANES)[:, None]
    n = jnp.arange(LANES)[None, :]
    distance = jnp.abs(k - HALF - n)
    b_re, b_im = (banded(t, distance, n < STEP) for t in (d_re, d_im))
    y_mat = jnp.concatenate(
        [jnp.concatenate([b_re, b_im], 2), jnp.concatenate([-b_im, b_re], 2)], 1
    )
    y_high, y_low = split(y_mat)
    return x_all, jnp.concatenate([y_high, y_high, y_low], 1)


def two_parts(x):
    high = x.astype(jnp.bfloat16)
    return high, (x - high.astype(jnp.float32)).astype(jnp.bfloat16)


def body(
    lat_size, source, receiver, zone, blend, x_mat, y_mat,
    image, field, halo, table, weights, xbuf, ybuf, part, arrived,
    load_sem, table_sem, table_sent, passed_sent, send_sem, recv_sem, part_sem, part_sent,
):
    own_levels, rows, cols = zone.shape
    levels, width_all = table.shape[1], table.shape[3]
    depths = levels // own_levels
    pairs = x_mat.shape[0]
    refs = y_mat.shape[1]
    half = part.shape[2]
    windows = -(-width_all // STEP)
    lat = lax.axis_index("lat")
    me = lax.axis_index("depth")
    side, core = me // 2, lax.rem(me, 2)
    has_up = lat > 0
    has_down = lat < lat_size - 1
    inner = pl.ds(PAD, width_all)

    def columns_of(device):
        return pl.ds(pl.multiple_of((device // 2) * (cols - width_all), LANES), width_all)

    peers = [side * 2 + 1 - core, (1 - side) * 2 + core, (1 - side) * 2 + 1 - core]
    tables = (zone, blend)

    loads = [
        pltpu.make_async_copy(
            ref.at[:, core * pairs + q, :, columns_of(me)],
            field.at[2 * q + f, :, :, inner],
            load_sem.at[2 * q + f],
        )
        for q in range(pairs)
        for f, ref in enumerate((source, receiver))
    ]
    for load in loads:
        load.start()

    def own_table(a, n):
        at = me * own_levels + n
        return pltpu.make_async_copy(
            tables[a].at[n, :, columns_of(me)], table.at[a, at], table_sem.at[a, at]
        )

    partner = peers[0]
    far_levels = 2 * own_levels

    def peer_table(across, a, n):
        at = me * own_levels + n
        peer = (1 - side) * 2 + a if across else partner
        return pltpu.make_async_remote_copy(
            src_ref=tables[a].at[n, :, columns_of(peer)],
            dst_ref=table.at[a, at],
            send_sem=table_sent.at[int(across), a, n],
            recv_sem=table_sem.at[a, at],
            device_id={"depth": peer},
        )

    def passed(i):
        at = (1 - side) * far_levels + i
        return pltpu.make_async_remote_copy(
            src_ref=table.at[core, at],
            dst_ref=table.at[core, at],
            send_sem=passed_sent.at[i],
            recv_sem=table_sem.at[core, at],
            device_id={"depth": partner},
        )

    def pass_on(i):
        at = (1 - side) * far_levels + i
        there = table.at[core, at]
        pltpu.make_async_copy(there, there, table_sem.at[core, at]).wait()
        passed(i).start()

    for n in range(own_levels):
        for a in range(2):
            own_table(a, n).start()
    halo[...] = jnp.zeros_like(halo)
    for s in range(2 * pairs):
        for c in range(2):
            field[s, c, :, 0:PAD] = jnp.zeros((rows, PAD), jnp.float32)
            field[s, c, :, PAD + width_all :] = jnp.zeros((rows, PAD), jnp.float32)

    barrier = pltpu.get_barrier_semaphore()

    @pl.when(has_up)
    def _():
        pl.semaphore_signal(barrier, inc=1, device_id={"lat": lat - 1})

    @pl.when(has_down)
    def _():
        pl.semaphore_signal(barrier, inc=1, device_id={"lat": lat + 1})

    for peer in peers:
        pl.semaphore_signal(barrier, inc=1, device_id={"depth": peer})
    pl.semaphore_wait(
        barrier, len(peers) + has_up.astype(jnp.int32) + has_down.astype(jnp.int32)
    )

    def to_up(s, slot):
        return pltpu.make_async_remote_copy(
            src_ref=field.at[s, :, pl.ds(0, HALO), inner],
            dst_ref=halo.at[slot, s, 1, :, :, inner],
            send_sem=send_sem.at[s, 0],
            recv_sem=recv_sem.at[slot, s, 1],
            device_id={"lat": lat - 1},
        )

    def to_down(s, slot):
        return pltpu.make_async_remote_copy(
            src_ref=field.at[s, :, pl.ds(rows - HALO, HALO), inner],
            dst_ref=halo.at[slot, s, 0, :, :, inner],
            send_sem=send_sem.at[s, 1],
            recv_sem=recv_sem.at[slot, s, 0],
            device_id={"lat": lat + 1},
        )

    def each_side(act_up, act_down):
        @pl.when(has_up)
        def _():
            act_up()

        @pl.when(has_down)
        def _():
            act_down()

    def send(s, slot):
        each_side(lambda: to_up(s, slot).start(), lambda: to_down(s, slot).start())

    def wait_sent(s, slot):
        each_side(lambda: to_up(s, slot).wait_send(), lambda: to_down(s, slot).wait_send())

    def wait_arrived(s, slot):
        each_side(lambda: to_down(s, slot).wait_recv(), lambda: to_up(s, slot).wait_recv())

    for s in range(2 * pairs):
        loads[s].wait()
        if s % 2 == 1:
            field[s, 1] = -field[s, 1]
        send(s, 0)
    for n in range(own_levels):
        @pl.when(core == 0)
        def _():
            for a in range(2):
                peer_table(True, a, n).start()

        for a in range(2):
            peer_table(False, a, n).start()
    for i in range(AHEAD):
        pass_on(i)

    def part_copy(z):
        return pltpu.make_async_remote_copy(
            src_ref=part.at[z],
            dst_ref=arrived.at[lax.rem(z, own_levels), me],
            send_sem=part_sent.at[z],
            recv_sem=part_sem.at[lax.rem(z, own_levels), me],
            device_id={"depth": z // own_levels},
        )

    def level(z, carry):
        slot = lax.rem(z, 2)

        @pl.when(jnp.logical_and(core == 1, z < own_levels))
        def _():
            for a in range(2):
                peer_table(True, a, z).start()

        @pl.when(z + AHEAD < far_levels)
        def _():
            pass_on(z + AHEAD)

        for a in range(2):
            taken = jnp.logical_and(z // far_levels != side, core == a)

            @pl.when(jnp.logical_not(taken))
            def _():
                pltpu.make_async_copy(table.at[a, z], table.at[a, z], table_sem.at[a, z]).wait()

        for w in range(windows):
            width = min(STEP, width_all - w * STEP)
            here = pl.ds(w * STEP, width)
            which = table[0, z, :, here]
            upper = table[1, z, :, here].astype(jnp.float32) * (1.0 / BLEND)
            lower = 1.0 - upper
            for j in range(refs):
                weights[j, w * rows : (w + 1) * rows, 0:width] = jnp.where(
                    which == j, lower, jnp.where(which == j - 1, upper, 0.0)
                )
        for s in range(2 * pairs):
            q = s // 2
            wait_arrived(s, slot)
            for w in range(windows):
                at = pl.ds(PAD + w * STEP - HALF, LANES)
                parts = []
                for group in range(rows // GROUP):
                    column = []
                    for c in range(2):
                        first = group * GROUP - HALO
                        pieces = []
                        if first < 0:
                            pieces.append(halo[slot, s, 0, c, :, at])
                        low, high = max(first, 0), min(first + 2 * GROUP, rows)
                        pieces.append(field[s, c, low:high, at])
                        if first + 2 * GROUP > rows:
                            pieces.append(halo[slot, s, 1, c, :, at])
                        column.append(jnp.concatenate(pieces, 0))
                    parts.append(jnp.concatenate(column, 0))
                high, low = two_parts(jnp.concatenate(parts, 1))
                out = jnp.dot(
                    x_mat[q],
                    jnp.concatenate([high, low, high], 0),
                    preferred_element_type=jnp.float32,
                )
                for p, values in enumerate(two_parts(out)):
                    for j in range(refs):
                        for c in range(2):
                            for group in range(rows // GROUP):
                                top = (j * 2 + c) * GROUP
                                left = group * LANES
                                xbuf[
                                    j,
                                    w * rows + group * GROUP : w * rows + (group + 1) * GROUP,
                                    (p * 2 + c) * LANES : (p * 2 + c + 1) * LANES,
                                ] = values[top : top + GROUP, left : left + LANES]
            wait_sent(s, slot)
            for j in range(refs):
                ybuf[j] = jnp.dot(
                    jnp.concatenate([xbuf[j], xbuf[j, :, 0 : 2 * LANES]], 1),
                    y_mat[q, j],
                    preferred_element_type=jnp.float32,
                )
            for w in range(windows):
                width = min(STEP, width_all - w * STEP)
                block = slice(w * rows, (w + 1) * rows)
                for c in range(2):
                    total = weights[0, block, 0:width] * ybuf[0, block, c * LANES : c * LANES + width]
                    for j in range(1, refs):
                        total = total + (
                            weights[j, block, 0:width]
                            * ybuf[j, block, c * LANES : c * LANES + width]
                        )
                    field[s, c, :, pl.ds(PAD + w * STEP, width)] = total

            @pl.when(z < levels - 1)
            def _():
                send(s, 1 - slot)

        mine = pl.ds(pl.multiple_of(PAD + side * (width_all - half), LANES), half)
        total = jnp.zeros((rows, half), jnp.float32)
        for q in range(pairs):
            total = total + field[2 * q, 0, :, mine] * field[2 * q + 1, 0, :, mine]
            total = total - field[2 * q, 1, :, mine] * field[2 * q + 1, 1, :, mine]

        @pl.when(z // own_levels == me)
        def _():
            arrived[lax.rem(z, own_levels), me] = total

        @pl.when(z // own_levels != me)
        def _():
            part[z] = total
            part_copy(z).start()

        return carry

    lax.fori_loop(0, levels, level, 0)

    for n in range(own_levels):
        for a in range(2):
            peer_table(False, a, n).wait_send()
            peer_table(True, a, n).wait_send()
    for i in range(far_levels):
        passed(i).wait_send()

    def sent(z, carry):
        @pl.when(z // own_levels != me)
        def _():
            part_copy(z).wait_send()

        return carry

    lax.fori_loop(0, levels, sent, 0)
    for n in range(own_levels):
        for d in range(depths):
            @pl.when(d != me)
            def _():
                pltpu.make_async_copy(
                    arrived.at[n, d], arrived.at[n, d], part_sem.at[n, d]
                ).wait()

        for h in range(depths // 2):
            image[n, :, h * half : (h + 1) * half] = (
                arrived[n, 2 * h] + arrived[n, 2 * h + 1]
            ) * (1.0 / (2 * pairs))


def migrate(lat_size, depths, source, receiver, zone, blend, x_mat, y_mat):
    own_levels, rows, cols = zone.shape
    levels = depths * own_levels
    pairs, refs = y_mat.shape[:2]
    streams = 2 * pairs
    half = cols // 2
    width = half + -(-HALF * levels // LANES) * LANES
    windows = -(-width // STEP)
    vmem = pl.BlockSpec(memory_space=pltpu.VMEM)
    hbm = pl.BlockSpec(memory_space=pl.ANY)
    wide = width + 2 * PAD
    dma = pltpu.SemaphoreType.DMA
    return pl.pallas_call(
        functools.partial(body, lat_size),
        out_shape=jax.ShapeDtypeStruct((own_levels, rows, cols), jnp.float32),
        in_specs=[hbm, hbm, hbm, hbm, vmem, vmem],
        out_specs=vmem,
        scratch_shapes=[
            pltpu.VMEM((streams, 2, rows, wide), jnp.float32),
            pltpu.VMEM((2, streams, 2, 2, HALO, wide), jnp.float32),
            pltpu.VMEM((2, levels, rows, width), jnp.int32),
            pltpu.VMEM((refs, windows * rows, LANES), jnp.float32),
            pltpu.VMEM((refs, windows * rows, 4 * LANES), jnp.bfloat16),
            pltpu.VMEM((refs, windows * rows, 2 * LANES), jnp.float32),
            pltpu.VMEM((levels, rows, half), jnp.float32),
            pltpu.VMEM((own_levels, depths, rows, half), jnp.float32),
            dma((streams,)),
            dma((2, levels)),
            dma((2, 2, own_levels)),
            dma((2 * own_levels,)),
            dma((streams, 2)),
            dma((2, streams, 2)),
            dma((own_levels, depths)),
            dma((levels,)),
        ],
        compiler_params=pltpu.CompilerParams(
            collective_id=0, has_side_effects=True, vmem_limit_bytes=60 * 2**20
        ),
    )(source, receiver, zone, blend, x_mat, y_mat)


def local(lat_size, source_field, receiver_field, zone_index, blend_weight, ref_velocity, frequencies):
    depths = lax.axis_size("depth")
    pairs = source_field.shape[1] // 2
    core = lax.rem(lax.axis_index("depth"), 2)
    chosen = lax.dynamic_slice_in_dim(frequencies, core * pairs, pairs)
    made = [matrices(chosen[q], ref_velocity) for q in range(pairs)]
    x_mat, y_mat = (jnp.stack(m) for m in zip(*made))
    return migrate(
        lat_size, depths, source_field, receiver_field, zone_index, blend_weight, x_mat, y_mat
    )


def solution(mesh):
    in_specs = (
        P(None, None, "lat", None),
        P(None, None, "lat", None),
        P("depth", "lat", None),
        P("depth", "lat", None),
        P(),
        P(),
    )
    out_specs = P("depth", "lat", None)
    return jax.shard_map(
        functools.partial(local, mesh.shape["lat"]),
        mesh=mesh, in_specs=in_specs, out_specs=out_specs, check_vma=False,
    )
```

```python
import functools
import math

import jax
import jax.numpy as jnp
from jax import lax
from jax.experimental import pallas as pl
from jax.experimental.pallas import tpu as pltpu
from jax.sharding import PartitionSpec as P

HALF = 7
BLEND = 16
LANES = 128
PAD = 128
STEP = LANES - 2 * HALF
HALO = 8
GROUP = 16
FAR = 16
AHEAD = 2

cell_width = 5.0
depth_step = 10.0
taper_width = 16.0


def kernels(frequency, ref_velocity):
    offsets = jnp.arange(0, HALF + 1, dtype=jnp.int32).astype(jnp.float32)
    wavenumber = 2.0 * math.pi * frequency.astype(jnp.float32) / ref_velocity
    curvature = wavenumber * (cell_width * cell_width / (2.0 * depth_step))
    phase_turn = wavenumber * depth_step
    chirp_angle = curvature[:, None] * (offsets * offsets)[None, :]
    envelope = jnp.exp(-offsets * offsets / taper_width)
    raw_re = envelope * jnp.cos(chirp_angle)
    raw_im = envelope * jnp.sin(chirp_angle)
    both = jnp.where(offsets == 0.0, 1.0, 2.0)
    magnitude = jnp.sqrt(
        jnp.sum(both * raw_re, axis=-1) ** 2 + jnp.sum(both * raw_im, axis=-1) ** 2
    )[:, None]
    return raw_re / magnitude, raw_im / magnitude, jnp.cos(phase_turn), jnp.sin(phase_turn)


def split(x):
    high = lax.reduce_precision(x, 8, 7)
    return high.astype(jnp.bfloat16), (x - high).astype(jnp.bfloat16)


def banded(taps, distance, keep):
    out = jnp.zeros((taps.shape[0],) + distance.shape, jnp.float32)
    for m in range(HALF + 1):
        out = jnp.where((distance == m) & keep, taps[:, m][:, None, None], out)
    return out


def matrices(frequency, ref_velocity):
    c_re, c_im, turn_cos, turn_sin = kernels(frequency, ref_velocity)
    refs = c_re.shape[0]
    r = jnp.arange(GROUP)[:, None]
    k = jnp.arange(2 * GROUP)[None, :]
    distance = jnp.abs(k - HALO - r)
    a_re, a_im = (banded(t, distance, True) for t in (c_re, c_im))
    x_mat = jnp.concatenate(
        [jnp.concatenate([a_re, -a_im], 2), jnp.concatenate([a_im, a_re], 2)], 1
    ).reshape(refs * 2 * GROUP, 4 * GROUP)
    x_high, x_low = split(x_mat)
    x_all = jnp.concatenate([x_high, x_high, x_low], 1)
    d_re = c_re * turn_cos[:, None] - c_im * turn_sin[:, None]
    d_im = c_re * turn_sin[:, None] + c_im * turn_cos[:, None]
    k = jnp.arange(LANES)[:, None]
    n = jnp.arange(LANES)[None, :]
    distance = jnp.abs(k - HALF - n)
    b_re, b_im = (banded(t, distance, n < STEP) for t in (d_re, d_im))
    y_mat = jnp.concatenate(
        [jnp.concatenate([b_re, b_im], 2), jnp.concatenate([-b_im, b_re], 2)], 1
    )
    y_high, y_low = split(y_mat)
    return x_all, jnp.concatenate([y_high, y_high, y_low], 1)


def two_parts(x):
    high = x.astype(jnp.bfloat16)
    return high, (x - high.astype(jnp.float32)).astype(jnp.bfloat16)


def body(
    lat_size, source, receiver, zone, blend, x_mat, y_mat,
    image, field, middle, halo, table, rim, weights, xbuf, ybuf, part, inbox, arrived,
    load_sem, table_sem, table_sent, passed_sent, rim_sem, rim_sent,
    send_sem, recv_sem, part_sem, part_sent, inbox_sem,
):
    own_levels, rows, cols = zone.shape
    levels, width_all = table.shape[1], table.shape[3]
    depths = levels // own_levels
    pairs = x_mat.shape[0]
    refs = y_mat.shape[1]
    half = part.shape[2]
    windows = -(-width_all // STEP)
    lat = lax.axis_index("lat")
    me = lax.axis_index("depth")
    side, core = me // 2, lax.rem(me, 2)
    has_up = lat > 0
    has_down = lat < lat_size - 1
    inner = pl.ds(PAD, width_all)

    def columns_of(device):
        return pl.ds(pl.multiple_of((device // 2) * (cols - width_all), LANES), width_all)

    peers = [side * 2 + 1 - core, (1 - side) * 2 + core, (1 - side) * 2 + 1 - core]
    tables = (zone, blend)

    loads = [
        pltpu.make_async_copy(
            ref.at[:, core * pairs + q, :, columns_of(me)],
            field.at[2 * q + f, :, :, inner],
            load_sem.at[2 * q + f],
        )
        for q in range(pairs)
        for f, ref in enumerate((source, receiver))
    ]
    for load in loads:
        load.start()

    def own_table(a, n):
        at = me * own_levels + n
        return pltpu.make_async_copy(
            tables[a].at[n, :, columns_of(me)], table.at[a, at], table_sem.at[a, at]
        )

    partner = peers[0]
    far_levels = 2 * own_levels

    def peer_table(across, a, n):
        at = me * own_levels + n
        peer = (1 - side) * 2 + a if across else partner
        return pltpu.make_async_remote_copy(
            src_ref=tables[a].at[n, :, columns_of(peer)],
            dst_ref=table.at[a, at],
            send_sem=table_sent.at[int(across), a, n],
            recv_sem=table_sem.at[a, at],
            device_id={"depth": peer},
        )

    def passed(i):
        at = (1 - side) * far_levels + i
        return pltpu.make_async_remote_copy(
            src_ref=table.at[core, at],
            dst_ref=table.at[core, at],
            send_sem=passed_sent.at[i],
            recv_sem=table_sem.at[core, at],
            device_id={"depth": partner},
        )

    def pass_on(i):
        at = (1 - side) * far_levels + i
        there = table.at[core, at]
        pltpu.make_async_copy(there, there, table_sem.at[core, at]).wait()
        passed(i).start()

    for n in range(own_levels):
        for a in range(2):
            own_table(a, n).start()
    halo[...] = jnp.zeros_like(halo)
    rim[...] = jnp.full(rim.shape, -2, jnp.int32)
    for ref in (field, middle):
        outside = jnp.zeros((ref.shape[2], PAD), jnp.float32)
        for s in range(2 * pairs):
            for c in range(2):
                ref[s, c, :, 0:PAD] = outside
                ref[s, c, :, PAD + width_all :] = outside

    barrier = pltpu.get_barrier_semaphore()

    @pl.when(has_up)
    def _():
        pl.semaphore_signal(barrier, inc=1, device_id={"lat": lat - 1})

    @pl.when(has_down)
    def _():
        pl.semaphore_signal(barrier, inc=1, device_id={"lat": lat + 1})

    for peer in peers:
        pl.semaphore_signal(barrier, inc=1, device_id={"depth": peer})
    pl.semaphore_wait(
        barrier, len(peers) + has_up.astype(jnp.int32) + has_down.astype(jnp.int32)
    )

    def to_up(s, slot, count):
        return pltpu.make_async_remote_copy(
            src_ref=field.at[s, :, pl.ds(0, count), inner],
            dst_ref=halo.at[slot, s, 1, :, pl.ds(0, count), inner],
            send_sem=send_sem.at[s, 0],
            recv_sem=recv_sem.at[slot, s, 1],
            device_id={"lat": lat - 1},
        )

    def to_down(s, slot, count):
        return pltpu.make_async_remote_copy(
            src_ref=field.at[s, :, pl.ds(rows - count, count), inner],
            dst_ref=halo.at[slot, s, 0, :, pl.ds(FAR - count, count), inner],
            send_sem=send_sem.at[s, 1],
            recv_sem=recv_sem.at[slot, s, 0],
            device_id={"lat": lat + 1},
        )

    def each_side(act_up, act_down):
        @pl.when(has_up)
        def _():
            act_up()

        @pl.when(has_down)
        def _():
            act_down()

    def send(s, slot, count):
        each_side(
            lambda: to_up(s, slot, count).start(), lambda: to_down(s, slot, count).start()
        )

    def wait_sent(s, slot, count):
        each_side(
            lambda: to_up(s, slot, count).wait_send(),
            lambda: to_down(s, slot, count).wait_send(),
        )

    def wait_arrived(s, slot, count):
        each_side(
            lambda: to_down(s, slot, count).wait_recv(),
            lambda: to_up(s, slot, count).wait_recv(),
        )

    def rim_up(h):
        return pltpu.make_async_remote_copy(
            src_ref=table.at[:, 2 * h, pl.ds(0, HALO)],
            dst_ref=rim.at[h, 1],
            send_sem=rim_sent.at[h, 0],
            recv_sem=rim_sem.at[h, 1],
            device_id={"lat": lat - 1},
        )

    def rim_down(h):
        return pltpu.make_async_remote_copy(
            src_ref=table.at[:, 2 * h, pl.ds(rows - HALO, HALO)],
            dst_ref=rim.at[h, 0],
            send_sem=rim_sent.at[h, 1],
            recv_sem=rim_sem.at[h, 0],
            device_id={"lat": lat + 1},
        )

    def need(z):
        for a in range(2):
            taken = jnp.logical_and(z // far_levels != side, core == a)

            @pl.when(jnp.logical_not(taken))
            def _():
                pltpu.make_async_copy(table.at[a, z], table.at[a, z], table_sem.at[a, z]).wait()

    for s in range(2 * pairs):
        loads[s].wait()
        if s % 2 == 1:
            field[s, 1] = -field[s, 1]
        send(s, 0, HALO)
    for n in range(own_levels):
        @pl.when(core == 0)
        def _():
            for a in range(2):
                peer_table(True, a, n).start()

        for a in range(2):
            peer_table(False, a, n).start()
    for i in range(AHEAD):
        pass_on(i)

    def part_copy(z):
        return pltpu.make_async_remote_copy(
            src_ref=part.at[z],
            dst_ref=arrived.at[lax.rem(z, own_levels), me],
            send_sem=part_sent.at[z],
            recv_sem=part_sem.at[lax.rem(z, own_levels), me],
            device_id={"depth": z // own_levels},
        )

    def set_weights(z, pieces):
        count = rows + (2 * HALO if pieces else 0)
        for w in range(windows):
            width = min(STEP, width_all - w * STEP)
            here = pl.ds(w * STEP, width)
            both = []
            for a in range(2):
                value = table[a, z, :, here]
                if pieces:
                    value = jnp.concatenate(
                        [rim[z // 2, 0, a, :, here], value, rim[z // 2, 1, a, :, here]], 0
                    )
                both.append(value)
            which = both[0]
            upper = both[1].astype(jnp.float32) * (1.0 / BLEND)
            lower = 1.0 - upper
            for j in range(refs):
                weights[int(pieces), j, w * count : (w + 1) * count, 0:width] = jnp.where(
                    which == j, lower, jnp.where(which == j - 1, upper, 0.0)
                )

    def advance(q, wide_step, read, before_write, target, s):
        groups = 3 if wide_step else 2
        count = groups * GROUP
        units = [(w, g) for w in range(windows) for g in range(groups)]
        for first in range(0, len(units), 2):
            chosen = units[first : first + 2]
            parts = []
            for w, g in chosen:
                at = pl.ds(PAD + w * STEP - HALF, LANES)
                parts.append(jnp.concatenate([read(c, g, at) for c in range(2)], 0))
            high, low = two_parts(jnp.concatenate(parts, 1))
            out = jnp.dot(
                x_mat[q],
                jnp.concatenate([high, low, high], 0),
                preferred_element_type=jnp.float32,
            )
            for p, values in enumerate(two_parts(out)):
                for j in range(refs):
                    for c in range(2):
                        for n, (w, g) in enumerate(chosen):
                            top = (j * 2 + c) * GROUP
                            row = w * count + g * GROUP
                            xbuf[
                                j,
                                row : row + GROUP,
                                (p * 2 + c) * LANES : (p * 2 + c + 1) * LANES,
                            ] = values[top : top + GROUP, n * LANES : (n + 1) * LANES]
        before_write()
        used = windows * count
        for j in range(refs):
            ybuf[j, 0:used] = jnp.dot(
                jnp.concatenate([xbuf[j, 0:used], xbuf[j, 0:used, 0 : 2 * LANES]], 1),
                y_mat[q, j],
                preferred_element_type=jnp.float32,
            )
        for w in range(windows):
            width = min(STEP, width_all - w * STEP)
            block = slice(w * count, (w + 1) * count)
            for c in range(2):
                total = None
                for j in range(refs):
                    term = (
                        weights[int(wide_step), j, block, 0:width]
                        * ybuf[j, block, c * LANES : c * LANES + width]
                    )
                    total = term if total is None else total + term
                target[s, c, :, pl.ds(PAD + w * STEP, width)] = total

    def to_partner(z):
        return pltpu.make_async_remote_copy(
            src_ref=part.at[z],
            dst_ref=inbox.at[lax.rem(z, far_levels)],
            send_sem=part_sent.at[z],
            recv_sem=inbox_sem.at[lax.rem(z, far_levels)],
            device_id={"depth": partner},
        )

    def image_of(z, ref, from_row):
        mine = pl.ds(pl.multiple_of(PAD + side * (width_all - half), LANES), half)
        taken = pl.ds(from_row, rows)
        total = jnp.zeros((rows, half), jnp.float32)
        for q in range(pairs):
            total = total + ref[2 * q, 0, taken, mine] * ref[2 * q + 1, 0, taken, mine]
            total = total - ref[2 * q, 1, taken, mine] * ref[2 * q + 1, 1, taken, mine]

        @pl.when(z // own_levels == me)
        def _():
            arrived[lax.rem(z, own_levels), me] = total

        @pl.when(z // own_levels != me)
        def _():
            part[z] = total

        @pl.when(jnp.logical_and(z // far_levels == side, z // own_levels != me))
        def _():
            part_copy(z).start()

        @pl.when(jnp.logical_and(z // far_levels != side, lax.rem(z, 2) != core))
        def _():
            to_partner(z).start()

    def finish(z):
        @pl.when(jnp.logical_and(z // far_levels != side, lax.rem(z, 2) == core))
        def _():
            to_partner(z).wait_recv()
            part[z] = part[z] + inbox[lax.rem(z, far_levels)]
            part_copy(z).start()

    single = levels // 2

    def one_level(z, carry):
        slot = lax.rem(z, 2)

        @pl.when(jnp.logical_and(core == 1, z < own_levels))
        def _():
            for a in range(2):
                peer_table(True, a, z).start()

        @pl.when(z + AHEAD < far_levels)
        def _():
            pass_on(z + AHEAD)

        need(z)
        set_weights(z, False)
        for s in range(2 * pairs):
            wait_arrived(s, slot, HALO)

            def read_field(c, g, at):
                if g == 0:
                    return jnp.concatenate(
                        [halo[slot, s, 0, c, FAR - HALO :, at], field[s, c, 0 : rows - HALO, at]], 0
                    )
                return jnp.concatenate(
                    [field[s, c, HALO:rows, at], halo[slot, s, 1, c, 0:HALO, at]], 0
                )

            advance(s // 2, False, read_field, lambda: wait_sent(s, slot, HALO), field, s)

            @pl.when(z < single - 1)
            def _():
                send(s, 1 - slot, HALO)

            @pl.when(z == single - 1)
            def _():
                send(s, 1 - slot, FAR)

        image_of(z, field, 0)

        @pl.when(z > 0)
        def _():
            finish(z - 1)

        return carry

    lax.fori_loop(0, single, one_level, 0)
    need(single)
    each_side(
        lambda: rim_up(single // 2).start(), lambda: rim_down(single // 2).start()
    )

    def two_levels(h, carry):
        slot = lax.rem(h, 2)
        z = 2 * h
        each_side(lambda: rim_down(h).wait_recv(), lambda: rim_up(h).wait_recv())
        set_weights(z, True)
        for s in range(2 * pairs):
            wait_arrived(s, slot, FAR)

            def read_wide(c, g, at):
                if g == 0:
                    return jnp.concatenate([halo[slot, s, 0, c, :, at], field[s, c, 0:FAR, at]], 0)
                if g == 1:
                    return field[s, c, :, at]
                return jnp.concatenate(
                    [field[s, c, rows - FAR : rows, at], halo[slot, s, 1, c, :, at]], 0
                )

            def read_middle(c, g, at):
                return middle[s, c, g * GROUP : (g + 2) * GROUP, at]

            advance(s // 2, True, read_wide, lambda: None, middle, s)
            if s == 0:
                need(z + 1)
                set_weights(z + 1, False)
            if s == 1:
                @pl.when(z + 2 < levels)
                def _():
                    need(z + 2)
                    each_side(lambda: rim_up(h + 1).start(), lambda: rim_down(h + 1).start())

            advance(s // 2, False, read_middle, lambda: wait_sent(s, slot, FAR), field, s)

            @pl.when(z + 2 < levels)
            def _():
                send(s, 1 - slot, FAR)

        image_of(z, middle, HALO)
        image_of(z + 1, field, 0)
        finish(z - 1)

        @pl.when(z > single)
        def _():
            finish(z - 2)

        return carry

    lax.fori_loop(single // 2, levels // 2, two_levels, 0)

    finish(levels - 2)
    finish(levels - 1)
    for h in range(single // 2, levels // 2):
        each_side(lambda: rim_up(h).wait_send(), lambda: rim_down(h).wait_send())
    for n in range(own_levels):
        for a in range(2):
            peer_table(False, a, n).wait_send()
            peer_table(True, a, n).wait_send()
    for i in range(far_levels):
        passed(i).wait_send()

    def sent(z, carry):
        @pl.when(z // own_levels != me)
        def _():
            part_copy(z).wait_send()

        return carry

    lax.fori_loop(0, levels, sent, 0)
    for n in range(own_levels):
        for d in range(depths):
            comes = jnp.logical_or(side == d // 2, d % 2 == n % 2)

            @pl.when(jnp.logical_and(d != me, comes))
            def _():
                pltpu.make_async_copy(
                    arrived.at[n, d], arrived.at[n, d], part_sem.at[n, d]
                ).wait()

        for h in range(depths // 2):
            there = slice(h * half, (h + 1) * half)

            @pl.when(side == h)
            def _():
                image[n, :, there] = (arrived[n, 2 * h] + arrived[n, 2 * h + 1]) * (
                    1.0 / (2 * pairs)
                )

            @pl.when(side != h)
            def _():
                image[n, :, there] = arrived[n, 2 * h + n % 2] * (1.0 / (2 * pairs))


def migrate(lat_size, depths, source, receiver, zone, blend, x_mat, y_mat):
    own_levels, rows, cols = zone.shape
    levels = depths * own_levels
    pairs, refs = y_mat.shape[:2]
    streams = 2 * pairs
    half = cols // 2
    width = half + -(-HALF * levels // LANES) * LANES
    windows = -(-width // STEP)
    vmem = pl.BlockSpec(memory_space=pltpu.VMEM)
    hbm = pl.BlockSpec(memory_space=pl.ANY)
    wide = width + 2 * PAD
    dma = pltpu.SemaphoreType.DMA
    return pl.pallas_call(
        functools.partial(body, lat_size),
        out_shape=jax.ShapeDtypeStruct((own_levels, rows, cols), jnp.float32),
        in_specs=[hbm, hbm, hbm, hbm, vmem, vmem],
        out_specs=vmem,
        scratch_shapes=[
            pltpu.VMEM((streams, 2, rows, wide), jnp.float32),
            pltpu.VMEM((streams, 2, rows + 2 * HALO, wide), jnp.float32),
            pltpu.VMEM((2, streams, 2, 2, FAR, wide), jnp.float32),
            pltpu.VMEM((2, levels, rows, width), jnp.int32),
            pltpu.VMEM((levels // 2, 2, 2, HALO, width), jnp.int32),
            pltpu.VMEM((2, refs, windows * (rows + 2 * HALO), LANES), jnp.float32),
            pltpu.VMEM((refs, windows * (rows + 2 * HALO), 4 * LANES), jnp.bfloat16),
            pltpu.VMEM((refs, windows * (rows + 2 * HALO), 2 * LANES), jnp.float32),
            pltpu.VMEM((levels, rows, half), jnp.float32),
            pltpu.VMEM((2 * own_levels, rows, half), jnp.float32),
            pltpu.VMEM((own_levels, depths, rows, half), jnp.float32),
            dma((streams,)),
            dma((2, levels)),
            dma((2, 2, own_levels)),
            dma((2 * own_levels,)),
            dma((levels // 2, 2)),
            dma((levels // 2, 2)),
            dma((streams, 2)),
            dma((2, streams, 2)),
            dma((own_levels, depths)),
            dma((levels,)),
            dma((2 * own_levels,)),
        ],
        compiler_params=pltpu.CompilerParams(
            collective_id=0, has_side_effects=True, vmem_limit_bytes=60 * 2**20
        ),
    )(source, receiver, zone, blend, x_mat, y_mat)


def local(lat_size, source_field, receiver_field, zone_index, blend_weight, ref_velocity, frequencies):
    depths = lax.axis_size("depth")
    pairs = source_field.shape[1] // 2
    core = lax.rem(lax.axis_index("depth"), 2)
    chosen = lax.dynamic_slice_in_dim(frequencies, core * pairs, pairs)
    made = [matrices(chosen[q], ref_velocity) for q in range(pairs)]
    x_mat, y_mat = (jnp.stack(m) for m in zip(*made))
    return migrate(
        lat_size, depths, source_field, receiver_field, zone_index, blend_weight, x_mat, y_mat
    )


def solution(mesh):
    in_specs = (
        P(None, None, "lat", None),
        P(None, None, "lat", None),
        P("depth", "lat", None),
        P("depth", "lat", None),
        P(),
        P(),
    )
    out_specs = P("depth", "lat", None)
    return jax.shard_map(
        functools.partial(local, mesh.shape["lat"]),
        mesh=mesh, in_specs=in_specs, out_specs=out_specs, check_vma=False,
    )
```

```python
import functools
import math

import jax
import jax.numpy as jnp
from jax import lax
from jax.experimental import pallas as pl
from jax.experimental.pallas import tpu as pltpu
from jax.sharding import PartitionSpec as P

HALF = 7
BLEND = 16
LANES = 128
PAD = 128
STEP = LANES - 2 * HALF
HALO = 8
GROUP = 16
FAR = 16
AHEAD = 2

cell_width = 5.0
depth_step = 10.0
taper_width = 16.0


def two_parts(x):
    high = x.astype(jnp.bfloat16)
    return high, (x - high.astype(jnp.float32)).astype(jnp.bfloat16)


def taps_of(frequency, velocity):
    shape = (8, LANES)
    lane = lax.broadcasted_iota(jnp.int32, shape, 1)
    wavenumber = jnp.full(shape, 2.0 * math.pi * frequency) / jnp.full(shape, velocity)
    curvature = wavenumber * (cell_width * cell_width / (2.0 * depth_step))
    phase_turn = wavenumber * depth_step
    offset = jnp.minimum(lane, HALF + 1).astype(jnp.float32)
    envelope = jnp.where(lane <= HALF, jnp.exp(-offset * offset / taper_width), 0.0)
    angle = curvature * (offset * offset)
    raw_re = envelope * jnp.cos(angle)
    raw_im = envelope * jnp.sin(angle)
    sides = jnp.where(lane == 0, 1.0, 2.0)
    sum_re = jnp.sum(sides * raw_re, axis=1, keepdims=True)
    sum_im = jnp.sum(sides * raw_im, axis=1, keepdims=True)
    magnitude = jnp.sqrt(sum_re * sum_re + sum_im * sum_im)
    c_re, c_im = raw_re / magnitude, raw_im / magnitude
    turn_cos, turn_sin = jnp.cos(phase_turn), jnp.sin(phase_turn)
    return c_re, c_im, c_re * turn_cos - c_im * turn_sin, c_re * turn_sin + c_im * turn_cos


def banded(taps, distance):
    out = jnp.zeros(distance.shape, jnp.float32)
    for m in range(HALF + 1):
        tap = jnp.broadcast_to(taps[0:1, m : m + 1], distance.shape)
        out = jnp.where(distance == m, tap, out)
    return out


def set_matrices(at, frequency, velocity, x_mat, y_mat):
    c_re, c_im, d_re, d_im = taps_of(frequency, velocity)
    shape = (GROUP, 12 * GROUP)
    lane = lax.broadcasted_iota(jnp.int32, shape, 1)
    row = lax.broadcasted_iota(jnp.int32, shape, 0)
    distance = jnp.abs(lax.rem(lane, 2 * GROUP) - HALO - row)
    a_re, a_im = banded(c_re, distance), banded(c_im, distance)
    from_re = lax.rem(lane, 4 * GROUP) < 2 * GROUP
    for c, value in enumerate(
        (jnp.where(from_re, a_re, -a_im), jnp.where(from_re, a_im, a_re))
    ):
        high = value.astype(jnp.bfloat16).astype(jnp.float32)
        x_mat[at, c * GROUP : (c + 1) * GROUP] = jnp.where(
            lane < 8 * GROUP, high, value - high
        ).astype(jnp.bfloat16)
    shape = (LANES, LANES)
    k = lax.broadcasted_iota(jnp.int32, shape, 0)
    n = lax.broadcasted_iota(jnp.int32, shape, 1)
    distance = jnp.where(n < STEP, jnp.abs(k - HALF - n), 2 * LANES)
    b_re, b_im = banded(d_re, distance), banded(d_im, distance)
    for c, pair in enumerate(((b_re, b_im), (-b_im, b_re))):
        for o, value in enumerate(pair):
            for p, part in enumerate((0, 0, 1)):
                y_mat[
                    at,
                    (2 * p + c) * LANES : (2 * p + c + 1) * LANES,
                    o * LANES : (o + 1) * LANES,
                ] = two_parts(value)[part]


def body(
    lat_size, refs, source, receiver, zone, blend, velocities, frequencies,
    image, x_mat, y_mat, field, middle, halo, table, rim, weights, xbuf, ybuf, part, inbox, arrived,
    load_sem, table_sem, table_sent, passed_sent, rim_sem, rim_sent,
    send_sem, recv_sem, part_sem, part_sent, inbox_sem,
):
    own_levels, rows, cols = zone.shape
    levels, width_all = table.shape[1], table.shape[3]
    depths = levels // own_levels
    pairs = y_mat.shape[0] // refs
    half = part.shape[2]
    windows = -(-width_all // STEP)
    lat = lax.axis_index("lat")
    me = lax.axis_index("depth")
    side, core = me // 2, lax.rem(me, 2)
    has_up = lat > 0
    has_down = lat < lat_size - 1
    inner = pl.ds(PAD, width_all)

    def columns_of(device):
        return pl.ds(pl.multiple_of((device // 2) * (cols - width_all), LANES), width_all)

    peers = [side * 2 + 1 - core, (1 - side) * 2 + core, (1 - side) * 2 + 1 - core]
    tables = (zone, blend)

    loads = [
        pltpu.make_async_copy(
            ref.at[:, core * pairs + q, :, columns_of(me)],
            field.at[2 * q + f, :, :, inner],
            load_sem.at[2 * q + f],
        )
        for q in range(pairs)
        for f, ref in enumerate((source, receiver))
    ]
    for load in loads:
        load.start()

    def own_table(a, n):
        at = me * own_levels + n
        return pltpu.make_async_copy(
            tables[a].at[n, :, columns_of(me)], table.at[a, at], table_sem.at[a, at]
        )

    partner = peers[0]
    far_levels = 2 * own_levels

    def peer_table(across, a, n):
        at = me * own_levels + n
        peer = (1 - side) * 2 + a if across else partner
        return pltpu.make_async_remote_copy(
            src_ref=tables[a].at[n, :, columns_of(peer)],
            dst_ref=table.at[a, at],
            send_sem=table_sent.at[int(across), a, n],
            recv_sem=table_sem.at[a, at],
            device_id={"depth": peer},
        )

    def passed(i):
        at = (1 - side) * far_levels + i
        return pltpu.make_async_remote_copy(
            src_ref=table.at[core, at],
            dst_ref=table.at[core, at],
            send_sem=passed_sent.at[i],
            recv_sem=table_sem.at[core, at],
            device_id={"depth": partner},
        )

    def pass_on(i):
        at = (1 - side) * far_levels + i
        there = table.at[core, at]
        pltpu.make_async_copy(there, there, table_sem.at[core, at]).wait()
        passed(i).start()

    for n in range(own_levels):
        for a in range(2):
            own_table(a, n).start()
    halo[...] = jnp.zeros_like(halo)
    rim[...] = jnp.full(rim.shape, -2, jnp.int32)
    for ref in (field, middle):
        outside = jnp.zeros((ref.shape[2], PAD), jnp.float32)
        for s in range(2 * pairs):
            for c in range(2):
                ref[s, c, :, 0:PAD] = outside
                ref[s, c, :, PAD + width_all :] = outside

    barrier = pltpu.get_barrier_semaphore()

    @pl.when(has_up)
    def _():
        pl.semaphore_signal(barrier, inc=1, device_id={"lat": lat - 1})

    @pl.when(has_down)
    def _():
        pl.semaphore_signal(barrier, inc=1, device_id={"lat": lat + 1})

    for peer in peers:
        pl.semaphore_signal(barrier, inc=1, device_id={"depth": peer})
    pl.semaphore_wait(
        barrier, len(peers) + has_up.astype(jnp.int32) + has_down.astype(jnp.int32)
    )

    def to_up(s, slot, count):
        return pltpu.make_async_remote_copy(
            src_ref=field.at[s, :, pl.ds(0, count), inner],
            dst_ref=halo.at[slot, s, 1, :, pl.ds(0, count), inner],
            send_sem=send_sem.at[s, 0],
            recv_sem=recv_sem.at[slot, s, 1],
            device_id={"lat": lat - 1},
        )

    def to_down(s, slot, count):
        return pltpu.make_async_remote_copy(
            src_ref=field.at[s, :, pl.ds(rows - count, count), inner],
            dst_ref=halo.at[slot, s, 0, :, pl.ds(FAR - count, count), inner],
            send_sem=send_sem.at[s, 1],
            recv_sem=recv_sem.at[slot, s, 0],
            device_id={"lat": lat + 1},
        )

    def each_side(act_up, act_down):
        @pl.when(has_up)
        def _():
            act_up()

        @pl.when(has_down)
        def _():
            act_down()

    def send(s, slot, count):
        each_side(
            lambda: to_up(s, slot, count).start(), lambda: to_down(s, slot, count).start()
        )

    def wait_sent(s, slot, count):
        each_side(
            lambda: to_up(s, slot, count).wait_send(),
            lambda: to_down(s, slot, count).wait_send(),
        )

    def wait_arrived(s, slot, count):
        each_side(
            lambda: to_down(s, slot, count).wait_recv(),
            lambda: to_up(s, slot, count).wait_recv(),
        )

    def rim_up(h):
        return pltpu.make_async_remote_copy(
            src_ref=table.at[:, 2 * h, pl.ds(0, HALO)],
            dst_ref=rim.at[h, 1],
            send_sem=rim_sent.at[h, 0],
            recv_sem=rim_sem.at[h, 1],
            device_id={"lat": lat - 1},
        )

    def rim_down(h):
        return pltpu.make_async_remote_copy(
            src_ref=table.at[:, 2 * h, pl.ds(rows - HALO, HALO)],
            dst_ref=rim.at[h, 0],
            send_sem=rim_sent.at[h, 1],
            recv_sem=rim_sem.at[h, 0],
            device_id={"lat": lat + 1},
        )

    def need(z):
        for a in range(2):
            taken = jnp.logical_and(z // far_levels != side, core == a)

            @pl.when(jnp.logical_not(taken))
            def _():
                pltpu.make_async_copy(table.at[a, z], table.at[a, z], table_sem.at[a, z]).wait()

    for s in range(2 * pairs):
        loads[s].wait()
        if s % 2 == 1:
            field[s, 1] = -field[s, 1]
        send(s, 0, HALO)
    for n in range(own_levels):
        @pl.when(core == 0)
        def _():
            for a in range(2):
                peer_table(True, a, n).start()

        for a in range(2):
            peer_table(False, a, n).start()

    def prepare(at, carry):
        set_matrices(
            at,
            frequencies[core * pairs + at // refs].astype(jnp.float32),
            velocities[lax.rem(at, refs)],
            x_mat,
            y_mat,
        )
        return carry

    lax.fori_loop(0, pairs * refs, prepare, 0)
    for i in range(AHEAD):
        pass_on(i)

    def part_copy(z):
        return pltpu.make_async_remote_copy(
            src_ref=part.at[z],
            dst_ref=arrived.at[lax.rem(z, own_levels), me],
            send_sem=part_sent.at[z],
            recv_sem=part_sem.at[lax.rem(z, own_levels), me],
            device_id={"depth": z // own_levels},
        )

    def set_weights(z, pieces):
        count = rows + (2 * HALO if pieces else 0)
        for w in range(windows):
            width = min(STEP, width_all - w * STEP)
            here = pl.ds(w * STEP, width)
            both = []
            for a in range(2):
                value = table[a, z, :, here]
                if pieces:
                    value = jnp.concatenate(
                        [rim[z // 2, 0, a, :, here], value, rim[z // 2, 1, a, :, here]], 0
                    )
                both.append(value)
            which = both[0]
            upper = both[1].astype(jnp.float32) * (1.0 / BLEND)
            lower = 1.0 - upper
            for j in range(refs):
                weights[int(pieces), j, w * count : (w + 1) * count, 0:width] = jnp.where(
                    which == j, lower, jnp.where(which == j - 1, upper, 0.0)
                )

    def advance(q, wide_step, read, before_write, target, s):
        groups = 3 if wide_step else 2
        count = groups * GROUP
        units = [(w, g) for w in range(windows) for g in range(groups)]
        for first in range(0, len(units), 2):
            chosen = units[first : first + 2]
            parts = []
            for w, g in chosen:
                at = pl.ds(PAD + w * STEP - HALF, LANES)
                parts.append(jnp.concatenate([read(c, g, at) for c in range(2)], 0))
            high, low = two_parts(jnp.concatenate(parts, 1))
            out = jnp.dot(
                x_mat[q * refs : (q + 1) * refs].reshape(2 * refs * GROUP, 12 * GROUP),
                jnp.concatenate([high, low, high], 0),
                preferred_element_type=jnp.float32,
            )
            for p, values in enumerate(two_parts(out)):
                for j in range(refs):
                    for c in range(2):
                        for n, (w, g) in enumerate(chosen):
                            top = (j * 2 + c) * GROUP
                            row = w * count + g * GROUP
                            xbuf[
                                j,
                                row : row + GROUP,
                                (p * 2 + c) * LANES : (p * 2 + c + 1) * LANES,
                            ] = values[top : top + GROUP, n * LANES : (n + 1) * LANES]
        before_write()
        used = windows * count
        for j in range(refs):
            ybuf[j, 0:used] = jnp.dot(
                jnp.concatenate([xbuf[j, 0:used], xbuf[j, 0:used, 0 : 2 * LANES]], 1),
                y_mat[q * refs + j],
                preferred_element_type=jnp.float32,
            )
        for w in range(windows):
            width = min(STEP, width_all - w * STEP)
            block = slice(w * count, (w + 1) * count)
            for c in range(2):
                total = None
                for j in range(refs):
                    term = (
                        weights[int(wide_step), j, block, 0:width]
                        * ybuf[j, block, c * LANES : c * LANES + width]
                    )
                    total = term if total is None else total + term
                target[s, c, :, pl.ds(PAD + w * STEP, width)] = total

    def to_partner(z):
        return pltpu.make_async_remote_copy(
            src_ref=part.at[z],
            dst_ref=inbox.at[lax.rem(z, far_levels)],
            send_sem=part_sent.at[z],
            recv_sem=inbox_sem.at[lax.rem(z, far_levels)],
            device_id={"depth": partner},
        )

    def image_of(z, ref, from_row):
        mine = pl.ds(pl.multiple_of(PAD + side * (width_all - half), LANES), half)
        taken = pl.ds(from_row, rows)
        total = jnp.zeros((rows, half), jnp.float32)
        for q in range(pairs):
            total = total + ref[2 * q, 0, taken, mine] * ref[2 * q + 1, 0, taken, mine]
            total = total - ref[2 * q, 1, taken, mine] * ref[2 * q + 1, 1, taken, mine]

        @pl.when(z // own_levels == me)
        def _():
            arrived[lax.rem(z, own_levels), me] = total

        @pl.when(z // own_levels != me)
        def _():
            part[z] = total

        @pl.when(jnp.logical_and(z // far_levels == side, z // own_levels != me))
        def _():
            part_copy(z).start()

        @pl.when(jnp.logical_and(z // far_levels != side, lax.rem(z, 2) != core))
        def _():
            to_partner(z).start()

    def finish(z):
        @pl.when(jnp.logical_and(z // far_levels != side, lax.rem(z, 2) == core))
        def _():
            to_partner(z).wait_recv()
            part[z] = part[z] + inbox[lax.rem(z, far_levels)]
            part_copy(z).start()

    single = own_levels

    def one_level(z, carry):
        slot = lax.rem(z, 2)

        @pl.when(jnp.logical_and(core == 1, z < own_levels))
        def _():
            for a in range(2):
                peer_table(True, a, z).start()

        @pl.when(z + AHEAD < far_levels)
        def _():
            pass_on(z + AHEAD)

        need(z)
        set_weights(z, False)
        for s in range(2 * pairs):
            wait_arrived(s, slot, HALO)

            def read_field(c, g, at):
                if g == 0:
                    return jnp.concatenate(
                        [halo[slot, s, 0, c, FAR - HALO :, at], field[s, c, 0 : rows - HALO, at]], 0
                    )
                return jnp.concatenate(
                    [field[s, c, HALO:rows, at], halo[slot, s, 1, c, 0:HALO, at]], 0
                )

            advance(s // 2, False, read_field, lambda: wait_sent(s, slot, HALO), field, s)

            @pl.when(z < single - 1)
            def _():
                send(s, 1 - slot, HALO)

            @pl.when(z == single - 1)
            def _():
                send(s, 1 - slot, FAR)

        image_of(z, field, 0)

        @pl.when(z > 0)
        def _():
            finish(z - 1)

        return carry

    lax.fori_loop(0, single, one_level, 0)
    need(single)
    each_side(
        lambda: rim_up(single // 2).start(), lambda: rim_down(single // 2).start()
    )

    def two_levels(h, carry):
        slot = lax.rem(h, 2)
        z = 2 * h
        each_side(lambda: rim_down(h).wait_recv(), lambda: rim_up(h).wait_recv())
        set_weights(z, True)
        for s in range(2 * pairs):
            wait_arrived(s, slot, FAR)

            def read_wide(c, g, at):
                if g == 0:
                    return jnp.concatenate([halo[slot, s, 0, c, :, at], field[s, c, 0:FAR, at]], 0)
                if g == 1:
                    return field[s, c, :, at]
                return jnp.concatenate(
                    [field[s, c, rows - FAR : rows, at], halo[slot, s, 1, c, :, at]], 0
                )

            def read_middle(c, g, at):
                return middle[s, c, g * GROUP : (g + 2) * GROUP, at]

            advance(s // 2, True, read_wide, lambda: None, middle, s)
            if s == 0:
                need(z + 1)
                set_weights(z + 1, False)
            if s % 2 == 1:
                @pl.when(z + s // 2 + AHEAD < far_levels)
                def _():
                    pass_on(z + s // 2 + AHEAD)

            if s == 1:
                @pl.when(z + 2 < levels)
                def _():
                    need(z + 2)
                    each_side(lambda: rim_up(h + 1).start(), lambda: rim_down(h + 1).start())

            advance(s // 2, False, read_middle, lambda: wait_sent(s, slot, FAR), field, s)

            @pl.when(z + 2 < levels)
            def _():
                send(s, 1 - slot, FAR)

        image_of(z, middle, HALO)
        image_of(z + 1, field, 0)
        finish(z - 1)

        @pl.when(z > single)
        def _():
            finish(z - 2)

        return carry

    lax.fori_loop(single // 2, levels // 2, two_levels, 0)

    finish(levels - 2)
    finish(levels - 1)
    for h in range(single // 2, levels // 2):
        each_side(lambda: rim_up(h).wait_send(), lambda: rim_down(h).wait_send())
    for n in range(own_levels):
        for a in range(2):
            peer_table(False, a, n).wait_send()
            peer_table(True, a, n).wait_send()
    for i in range(far_levels):
        passed(i).wait_send()

    def sent(z, carry):
        @pl.when(z // own_levels != me)
        def _():
            part_copy(z).wait_send()

        return carry

    lax.fori_loop(0, levels, sent, 0)
    for n in range(own_levels):
        for d in range(depths):
            comes = jnp.logical_or(side == d // 2, d % 2 == n % 2)

            @pl.when(jnp.logical_and(d != me, comes))
            def _():
                pltpu.make_async_copy(
                    arrived.at[n, d], arrived.at[n, d], part_sem.at[n, d]
                ).wait()

        for h in range(depths // 2):
            there = slice(h * half, (h + 1) * half)

            @pl.when(side == h)
            def _():
                image[n, :, there] = (arrived[n, 2 * h] + arrived[n, 2 * h + 1]) * (
                    1.0 / (2 * pairs)
                )

            @pl.when(side != h)
            def _():
                image[n, :, there] = arrived[n, 2 * h + n % 2] * (1.0 / (2 * pairs))


def migrate(lat_size, depths, source, receiver, zone, blend, velocities, frequencies):
    own_levels, rows, cols = zone.shape
    levels = depths * own_levels
    refs = velocities.shape[0]
    pairs = frequencies.shape[0] // 2
    streams = 2 * pairs
    half = cols // 2
    width = half + -(-HALF * levels // LANES) * LANES
    windows = -(-width // STEP)
    vmem = pl.BlockSpec(memory_space=pltpu.VMEM)
    smem = pl.BlockSpec(memory_space=pltpu.SMEM)
    hbm = pl.BlockSpec(memory_space=pl.ANY)
    wide = width + 2 * PAD
    dma = pltpu.SemaphoreType.DMA
    return pl.pallas_call(
        functools.partial(body, lat_size, refs),
        out_shape=jax.ShapeDtypeStruct((own_levels, rows, cols), jnp.float32),
        in_specs=[hbm, hbm, hbm, hbm, smem, smem],
        out_specs=vmem,
        scratch_shapes=[
            pltpu.VMEM((pairs * refs, 2 * GROUP, 12 * GROUP), jnp.bfloat16),
            pltpu.VMEM((pairs * refs, 6 * LANES, 2 * LANES), jnp.bfloat16),
            pltpu.VMEM((streams, 2, rows, wide), jnp.float32),
            pltpu.VMEM((streams, 2, rows + 2 * HALO, wide), jnp.float32),
            pltpu.VMEM((2, streams, 2, 2, FAR, wide), jnp.float32),
            pltpu.VMEM((2, levels, rows, width), jnp.int32),
            pltpu.VMEM((levels // 2, 2, 2, HALO, width), jnp.int32),
            pltpu.VMEM((2, refs, windows * (rows + 2 * HALO), LANES), jnp.float32),
            pltpu.VMEM((refs, windows * (rows + 2 * HALO), 4 * LANES), jnp.bfloat16),
            pltpu.VMEM((refs, windows * (rows + 2 * HALO), 2 * LANES), jnp.float32),
            pltpu.VMEM((levels, rows, half), jnp.float32),
            pltpu.VMEM((2 * own_levels, rows, half), jnp.float32),
            pltpu.VMEM((own_levels, depths, rows, half), jnp.float32),
            dma((streams,)),
            dma((2, levels)),
            dma((2, 2, own_levels)),
            dma((2 * own_levels,)),
            dma((levels // 2, 2)),
            dma((levels // 2, 2)),
            dma((streams, 2)),
            dma((2, streams, 2)),
            dma((own_levels, depths)),
            dma((levels,)),
            dma((2 * own_levels,)),
        ],
        compiler_params=pltpu.CompilerParams(
            collective_id=0, has_side_effects=True, vmem_limit_bytes=60 * 2**20
        ),
    )(source, receiver, zone, blend, velocities, frequencies)


def local(lat_size, source_field, receiver_field, zone_index, blend_weight, ref_velocity, frequencies):
    return migrate(
        lat_size, lax.axis_size("depth"), source_field, receiver_field, zone_index,
        blend_weight, ref_velocity, frequencies,
    )


def solution(mesh):
    in_specs = (
        P(None, None, "lat", None),
        P(None, None, "lat", None),
        P("depth", "lat", None),
        P("depth", "lat", None),
        P(),
        P(),
    )
    out_specs = P("depth", "lat", None)
    return jax.shard_map(
        functools.partial(local, mesh.shape["lat"]),
        mesh=mesh, in_specs=in_specs, out_specs=out_specs, check_vma=False,
    )
```

```python
import functools
import math

import jax
import jax.numpy as jnp
from jax import lax
from jax.experimental import pallas as pl
from jax.experimental.pallas import tpu as pltpu
from jax.sharding import PartitionSpec as P

HALF = 7
BLEND = 16
LANES = 128
PAD = 128
STEP = LANES - 2 * HALF
HALO = 8
GROUP = 16
FAR = 16
AHEAD = 2

cell_width = 5.0
depth_step = 10.0
taper_width = 16.0


def two_parts(x):
    high = x.astype(jnp.bfloat16)
    return high, (x - high.astype(jnp.float32)).astype(jnp.bfloat16)


def taps_of(frequency, velocity):
    shape = (8, LANES)
    lane = lax.broadcasted_iota(jnp.int32, shape, 1)
    wavenumber = jnp.full(shape, 2.0 * math.pi * frequency) / jnp.full(shape, velocity)
    curvature = wavenumber * (cell_width * cell_width / (2.0 * depth_step))
    phase_turn = wavenumber * depth_step
    offset = jnp.minimum(lane, HALF + 1).astype(jnp.float32)
    envelope = jnp.where(lane <= HALF, jnp.exp(-offset * offset / taper_width), 0.0)
    angle = curvature * (offset * offset)
    raw_re = envelope * jnp.cos(angle)
    raw_im = envelope * jnp.sin(angle)
    sides = jnp.where(lane == 0, 1.0, 2.0)
    sum_re = jnp.sum(sides * raw_re, axis=1, keepdims=True)
    sum_im = jnp.sum(sides * raw_im, axis=1, keepdims=True)
    magnitude = jnp.sqrt(sum_re * sum_re + sum_im * sum_im)
    c_re, c_im = raw_re / magnitude, raw_im / magnitude
    turn_cos, turn_sin = jnp.cos(phase_turn), jnp.sin(phase_turn)
    return c_re, c_im, c_re * turn_cos - c_im * turn_sin, c_re * turn_sin + c_im * turn_cos


def banded(taps, distance):
    out = jnp.zeros(distance.shape, jnp.float32)
    for m in range(HALF + 1):
        tap = jnp.broadcast_to(taps[0:1, m : m + 1], distance.shape)
        out = jnp.where(distance == m, tap, out)
    return out


def set_matrices(at, frequency, velocity, x_mat, y_mat):
    c_re, c_im, d_re, d_im = taps_of(frequency, velocity)
    shape = (GROUP, 12 * GROUP)
    lane = lax.broadcasted_iota(jnp.int32, shape, 1)
    row = lax.broadcasted_iota(jnp.int32, shape, 0)
    distance = jnp.abs(lax.rem(lane, 2 * GROUP) - HALO - row)
    a_re, a_im = banded(c_re, distance), banded(c_im, distance)
    from_re = lax.rem(lane, 4 * GROUP) < 2 * GROUP
    for c, value in enumerate(
        (jnp.where(from_re, a_re, -a_im), jnp.where(from_re, a_im, a_re))
    ):
        high = value.astype(jnp.bfloat16).astype(jnp.float32)
        x_mat[at, c * GROUP : (c + 1) * GROUP] = jnp.where(
            lane < 8 * GROUP, high, value - high
        ).astype(jnp.bfloat16)
    shape = (LANES, LANES)
    k = lax.broadcasted_iota(jnp.int32, shape, 0)
    n = lax.broadcasted_iota(jnp.int32, shape, 1)
    distance = jnp.where(n < STEP, jnp.abs(k - HALF - n), 2 * LANES)
    b_re, b_im = banded(d_re, distance), banded(d_im, distance)
    for c, pair in enumerate(((b_re, b_im), (-b_im, b_re))):
        for o, value in enumerate(pair):
            for p, part in enumerate((0, 0, 1)):
                y_mat[
                    at,
                    (2 * p + c) * LANES : (2 * p + c + 1) * LANES,
                    o * LANES : (o + 1) * LANES,
                ] = two_parts(value)[part]


def body(
    lat_size, refs, source, receiver, zone, blend, velocities, frequencies,
    image, x_mat, y_mat, field, middle, halo, table, rim, weights, xbuf, ybuf, part, inbox, arrived,
    load_sem, table_sem, table_sent, passed_sent, rim_sem, rim_sent,
    send_sem, recv_sem, part_sem, part_sent, inbox_sem,
):
    own_levels, rows, cols = zone.shape
    levels, width_all = table.shape[1], table.shape[3]
    depths = levels // own_levels
    pairs = y_mat.shape[0] // refs
    half = part.shape[2]
    windows = -(-width_all // STEP)
    lat = lax.axis_index("lat")
    me = lax.axis_index("depth")
    side, core = me // 2, lax.rem(me, 2)
    has_up = lat > 0
    has_down = lat < lat_size - 1
    inner = pl.ds(PAD, width_all)

    def columns_of(device):
        return pl.ds(pl.multiple_of((device // 2) * (cols - width_all), LANES), width_all)

    peers = [side * 2 + 1 - core, (1 - side) * 2 + core, (1 - side) * 2 + 1 - core]
    tables = (zone, blend)

    loads = [
        pltpu.make_async_copy(
            ref.at[:, core * pairs + q, :, columns_of(me)],
            field.at[2 * q + f, :, :, inner],
            load_sem.at[2 * q + f],
        )
        for q in range(pairs)
        for f, ref in enumerate((source, receiver))
    ]
    for load in loads:
        load.start()

    def own_table(a, n):
        at = me * own_levels + n
        return pltpu.make_async_copy(
            tables[a].at[n, :, columns_of(me)], table.at[a, at], table_sem.at[a, at]
        )

    partner = peers[0]
    far_levels = 2 * own_levels

    def peer_table(across, a, n):
        at = me * own_levels + n
        peer = (1 - side) * 2 + a if across else partner
        return pltpu.make_async_remote_copy(
            src_ref=tables[a].at[n, :, columns_of(peer)],
            dst_ref=table.at[a, at],
            send_sem=table_sent.at[int(across), a, n],
            recv_sem=table_sem.at[a, at],
            device_id={"depth": peer},
        )

    def passed(i):
        at = (1 - side) * far_levels + i
        return pltpu.make_async_remote_copy(
            src_ref=table.at[core, at],
            dst_ref=table.at[core, at],
            send_sem=passed_sent.at[i],
            recv_sem=table_sem.at[core, at],
            device_id={"depth": partner},
        )

    def pass_on(i):
        at = (1 - side) * far_levels + i
        there = table.at[core, at]
        pltpu.make_async_copy(there, there, table_sem.at[core, at]).wait()
        passed(i).start()

    for n in range(own_levels):
        for a in range(2):
            own_table(a, n).start()
    halo[...] = jnp.zeros_like(halo)
    rim[...] = jnp.full(rim.shape, -2, jnp.int32)
    for ref in (field, middle):
        outside = jnp.zeros((ref.shape[2], PAD), jnp.float32)
        for s in range(2 * pairs):
            for c in range(2):
                ref[s, c, :, 0:PAD] = outside
                ref[s, c, :, PAD + width_all :] = outside

    barrier = pltpu.get_barrier_semaphore()

    @pl.when(has_up)
    def _():
        pl.semaphore_signal(barrier, inc=1, device_id={"lat": lat - 1})

    @pl.when(has_down)
    def _():
        pl.semaphore_signal(barrier, inc=1, device_id={"lat": lat + 1})

    for peer in peers:
        pl.semaphore_signal(barrier, inc=1, device_id={"depth": peer})
    pl.semaphore_wait(
        barrier, len(peers) + has_up.astype(jnp.int32) + has_down.astype(jnp.int32)
    )

    def to_up(s, slot, count):
        return pltpu.make_async_remote_copy(
            src_ref=field.at[s, :, pl.ds(0, count), inner],
            dst_ref=halo.at[slot, s, 1, :, pl.ds(0, count), inner],
            send_sem=send_sem.at[s, 0],
            recv_sem=recv_sem.at[slot, s, 1],
            device_id={"lat": lat - 1},
        )

    def to_down(s, slot, count):
        return pltpu.make_async_remote_copy(
            src_ref=field.at[s, :, pl.ds(rows - count, count), inner],
            dst_ref=halo.at[slot, s, 0, :, pl.ds(FAR - count, count), inner],
            send_sem=send_sem.at[s, 1],
            recv_sem=recv_sem.at[slot, s, 0],
            device_id={"lat": lat + 1},
        )

    def each_side(act_up, act_down):
        @pl.when(has_up)
        def _():
            act_up()

        @pl.when(has_down)
        def _():
            act_down()

    def send(s, slot, count):
        each_side(
            lambda: to_up(s, slot, count).start(), lambda: to_down(s, slot, count).start()
        )

    def wait_sent(s, slot, count):
        each_side(
            lambda: to_up(s, slot, count).wait_send(),
            lambda: to_down(s, slot, count).wait_send(),
        )

    def wait_arrived(s, slot, count):
        each_side(
            lambda: to_down(s, slot, count).wait_recv(),
            lambda: to_up(s, slot, count).wait_recv(),
        )

    def rim_up(h):
        return pltpu.make_async_remote_copy(
            src_ref=table.at[:, 2 * h, pl.ds(0, HALO)],
            dst_ref=rim.at[h, 1],
            send_sem=rim_sent.at[h, 0],
            recv_sem=rim_sem.at[h, 1],
            device_id={"lat": lat - 1},
        )

    def rim_down(h):
        return pltpu.make_async_remote_copy(
            src_ref=table.at[:, 2 * h, pl.ds(rows - HALO, HALO)],
            dst_ref=rim.at[h, 0],
            send_sem=rim_sent.at[h, 1],
            recv_sem=rim_sem.at[h, 0],
            device_id={"lat": lat + 1},
        )

    def need(z):
        for a in range(2):
            taken = jnp.logical_and(z // far_levels != side, core == a)

            @pl.when(jnp.logical_not(taken))
            def _():
                pltpu.make_async_copy(table.at[a, z], table.at[a, z], table_sem.at[a, z]).wait()

    for s in range(2 * pairs):
        loads[s].wait()
        if s % 2 == 1:
            field[s, 1] = -field[s, 1]
        send(s, 0, HALO)
    for n in range(own_levels):
        @pl.when(core == 0)
        def _():
            for a in range(2):
                peer_table(True, a, n).start()

        for a in range(2):
            peer_table(False, a, n).start()

    def prepare(at, carry):
        set_matrices(
            at,
            frequencies[core * pairs + at // refs].astype(jnp.float32),
            velocities[lax.rem(at, refs)],
            x_mat,
            y_mat,
        )
        return carry

    lax.fori_loop(0, pairs * refs, prepare, 0)
    for i in range(AHEAD):
        pass_on(i)

    def part_copy(z):
        return pltpu.make_async_remote_copy(
            src_ref=part.at[z],
            dst_ref=arrived.at[lax.rem(z, own_levels), me],
            send_sem=part_sent.at[z],
            recv_sem=part_sem.at[lax.rem(z, own_levels), me],
            device_id={"depth": z // own_levels},
        )

    def set_weights(z, pieces):
        count = rows + (2 * HALO if pieces else 0)
        for w in range(windows):
            width = min(STEP, width_all - w * STEP)
            here = pl.ds(w * STEP, width)
            both = []
            for a in range(2):
                value = table[a, z, :, here]
                if pieces:
                    value = jnp.concatenate(
                        [rim[z // 2, 0, a, :, here], value, rim[z // 2, 1, a, :, here]], 0
                    )
                both.append(value)
            which = both[0]
            upper = both[1].astype(jnp.float32) * (1.0 / BLEND)
            lower = 1.0 - upper
            for j in range(refs):
                weights[int(pieces), j, w * count : (w + 1) * count, 0:width] = jnp.where(
                    which == j, lower, jnp.where(which == j - 1, upper, 0.0)
                )

    def advance(q, wide_step, read, before_write, target, streams):
        groups = 3 if wide_step else 2
        count = groups * GROUP
        used = windows * count
        split = {}
        units = [(i, w, g) for i in range(len(streams)) for w in range(windows) for g in range(groups)]
        for first in range(0, len(units), 2):
            chosen = units[first : first + 2]
            highs, lows = [], []
            for i, w, g in chosen:
                if (i, w) not in split:
                    at = pl.ds(PAD + w * STEP - HALF, LANES)
                    split[i, w] = [two_parts(read(streams[i], c, at)) for c in range(2)]
                taken = slice(g * GROUP, (g + 2) * GROUP)
                highs.append(jnp.concatenate([both[0][taken] for both in split[i, w]], 0))
                lows.append(jnp.concatenate([both[1][taken] for both in split[i, w]], 0))
            high, low = jnp.concatenate(highs, 1), jnp.concatenate(lows, 1)
            out = jnp.dot(
                x_mat[q * refs : (q + 1) * refs].reshape(2 * refs * GROUP, 12 * GROUP),
                jnp.concatenate([high, low, high], 0),
                preferred_element_type=jnp.float32,
            )
            for p, values in enumerate(two_parts(out)):
                for j in range(refs):
                    for c in range(2):
                        for n, (i, w, g) in enumerate(chosen):
                            top = (j * 2 + c) * GROUP
                            row = i * used + w * count + g * GROUP
                            xbuf[
                                j,
                                row : row + GROUP,
                                (p * 2 + c) * LANES : (p * 2 + c + 1) * LANES,
                            ] = values[top : top + GROUP, n * LANES : (n + 1) * LANES]
        before_write()
        every = len(streams) * used
        for j in range(refs):
            ybuf[j, 0:every] = jnp.dot(
                jnp.concatenate([xbuf[j, 0:every], xbuf[j, 0:every, 0 : 2 * LANES]], 1),
                y_mat[q * refs + j],
                preferred_element_type=jnp.float32,
            )
        for i, s in enumerate(streams):
            for w in range(windows):
                width = min(STEP, width_all - w * STEP)
                block = slice(w * count, (w + 1) * count)
                made = slice(i * used + w * count, i * used + (w + 1) * count)
                for c in range(2):
                    total = None
                    for j in range(refs):
                        term = (
                            weights[int(wide_step), j, block, 0:width]
                            * ybuf[j, made, c * LANES : c * LANES + width]
                        )
                        total = term if total is None else total + term
                    target[s, c, :, pl.ds(PAD + w * STEP, width)] = total

    def to_partner(z):
        return pltpu.make_async_remote_copy(
            src_ref=part.at[z],
            dst_ref=inbox.at[lax.rem(z, far_levels)],
            send_sem=part_sent.at[z],
            recv_sem=inbox_sem.at[lax.rem(z, far_levels)],
            device_id={"depth": partner},
        )

    def image_of(z, ref, from_row):
        mine = pl.ds(pl.multiple_of(PAD + side * (width_all - half), LANES), half)
        taken = pl.ds(from_row, rows)
        total = jnp.zeros((rows, half), jnp.float32)
        for q in range(pairs):
            total = total + ref[2 * q, 0, taken, mine] * ref[2 * q + 1, 0, taken, mine]
            total = total - ref[2 * q, 1, taken, mine] * ref[2 * q + 1, 1, taken, mine]

        @pl.when(z // own_levels == me)
        def _():
            arrived[lax.rem(z, own_levels), me] = total

        @pl.when(z // own_levels != me)
        def _():
            part[z] = total

        @pl.when(jnp.logical_and(z // far_levels == side, z // own_levels != me))
        def _():
            part_copy(z).start()

        @pl.when(jnp.logical_and(z // far_levels != side, lax.rem(z, 2) != core))
        def _():
            to_partner(z).start()

    def finish(z):
        @pl.when(jnp.logical_and(z // far_levels != side, lax.rem(z, 2) == core))
        def _():
            to_partner(z).wait_recv()
            part[z] = part[z] + inbox[lax.rem(z, far_levels)]
            part_copy(z).start()

    single = 2

    def one_level(z, carry):
        slot = lax.rem(z, 2)

        @pl.when(jnp.logical_and(core == 1, 2 * z < own_levels))
        def _():
            for n in range(2):
                for a in range(2):
                    peer_table(True, a, 2 * z + n).start()

        @pl.when(z + AHEAD < far_levels)
        def _():
            pass_on(z + AHEAD)

        need(z)
        set_weights(z, False)
        for s in range(2 * pairs):
            wait_arrived(s, slot, HALO)

            def read_field(s, c, at):
                return jnp.concatenate(
                    [
                        halo[slot, s, 0, c, FAR - HALO :, at],
                        field[s, c, :, at],
                        halo[slot, s, 1, c, 0:HALO, at],
                    ],
                    0,
                )

            advance(s // 2, False, read_field, lambda: wait_sent(s, slot, HALO), field, [s])

            @pl.when(z < single - 1)
            def _():
                send(s, 1 - slot, HALO)

            @pl.when(z == single - 1)
            def _():
                send(s, 1 - slot, FAR)

        image_of(z, field, 0)

        @pl.when(z > 0)
        def _():
            finish(z - 1)

        return carry

    lax.fori_loop(0, single, one_level, 0)
    need(single)
    each_side(
        lambda: rim_up(single // 2).start(), lambda: rim_down(single // 2).start()
    )

    def two_levels(h, carry):
        slot = lax.rem(h - single // 2, 2)
        z = 2 * h
        each_side(lambda: rim_down(h).wait_recv(), lambda: rim_up(h).wait_recv())
        set_weights(z, True)

        def read_wide(s, c, at):
            return jnp.concatenate(
                [halo[slot, s, 0, c, :, at], field[s, c, :, at], halo[slot, s, 1, c, :, at]], 0
            )

        def read_middle(s, c, at):
            return middle[s, c, :, at]

        for streams in ([0], [1], [2], [3]):
            q = streams[0] // 2

            def all_sent():
                for s in streams:
                    wait_sent(s, slot, FAR)

            for s in streams:
                wait_arrived(s, slot, FAR)
            advance(q, True, read_wide, lambda: None, middle, streams)
            if streams[0] == 0:
                need(z + 1)
                set_weights(z + 1, False)
                for ahead in range(AHEAD, 2 * AHEAD):
                    @pl.when(z + ahead < far_levels)
                    def _():
                        pass_on(z + ahead)

            if streams[-1] == 1:
                @pl.when(z + 2 < levels)
                def _():
                    need(z + 2)
                    each_side(lambda: rim_up(h + 1).start(), lambda: rim_down(h + 1).start())

            advance(q, False, read_middle, all_sent, field, streams)

            @pl.when(z + 2 < levels)
            def _():
                for s in streams:
                    send(s, 1 - slot, FAR)

        image_of(z, middle, HALO)
        image_of(z + 1, field, 0)
        finish(z - 1)

        @pl.when(z > single)
        def _():
            finish(z - 2)

        return carry

    lax.fori_loop(single // 2, levels // 2, two_levels, 0)

    finish(levels - 2)
    finish(levels - 1)
    for h in range(single // 2, levels // 2):
        each_side(lambda: rim_up(h).wait_send(), lambda: rim_down(h).wait_send())
    for n in range(own_levels):
        for a in range(2):
            peer_table(False, a, n).wait_send()
            peer_table(True, a, n).wait_send()
    for i in range(far_levels):
        passed(i).wait_send()

    def sent(z, carry):
        @pl.when(z // own_levels != me)
        def _():
            part_copy(z).wait_send()

        return carry

    lax.fori_loop(0, levels, sent, 0)
    for n in range(own_levels):
        for d in range(depths):
            comes = jnp.logical_or(side == d // 2, d % 2 == n % 2)

            @pl.when(jnp.logical_and(d != me, comes))
            def _():
                pltpu.make_async_copy(
                    arrived.at[n, d], arrived.at[n, d], part_sem.at[n, d]
                ).wait()

        for h in range(depths // 2):
            there = slice(h * half, (h + 1) * half)

            @pl.when(side == h)
            def _():
                image[n, :, there] = (arrived[n, 2 * h] + arrived[n, 2 * h + 1]) * (
                    1.0 / (2 * pairs)
                )

            @pl.when(side != h)
            def _():
                image[n, :, there] = arrived[n, 2 * h + n % 2] * (1.0 / (2 * pairs))


def migrate(lat_size, depths, source, receiver, zone, blend, velocities, frequencies):
    own_levels, rows, cols = zone.shape
    levels = depths * own_levels
    refs = velocities.shape[0]
    pairs = frequencies.shape[0] // 2
    streams = 2 * pairs
    half = cols // 2
    width = half + -(-HALF * levels // LANES) * LANES
    windows = -(-width // STEP)
    vmem = pl.BlockSpec(memory_space=pltpu.VMEM)
    smem = pl.BlockSpec(memory_space=pltpu.SMEM)
    hbm = pl.BlockSpec(memory_space=pl.ANY)
    wide = width + 2 * PAD
    dma = pltpu.SemaphoreType.DMA
    return pl.pallas_call(
        functools.partial(body, lat_size, refs),
        out_shape=jax.ShapeDtypeStruct((own_levels, rows, cols), jnp.float32),
        in_specs=[hbm, hbm, hbm, hbm, smem, smem],
        out_specs=vmem,
        scratch_shapes=[
            pltpu.VMEM((pairs * refs, 2 * GROUP, 12 * GROUP), jnp.bfloat16),
            pltpu.VMEM((pairs * refs, 6 * LANES, 2 * LANES), jnp.bfloat16),
            pltpu.VMEM((streams, 2, rows, wide), jnp.float32),
            pltpu.VMEM((streams, 2, rows + 2 * HALO, wide), jnp.float32),
            pltpu.VMEM((2, streams, 2, 2, FAR, wide), jnp.float32),
            pltpu.VMEM((2, levels, rows, width), jnp.int32),
            pltpu.VMEM((levels // 2, 2, 2, HALO, width), jnp.int32),
            pltpu.VMEM((2, refs, windows * (rows + 2 * HALO), LANES), jnp.float32),
            pltpu.VMEM((refs, 2 * windows * (rows + 2 * HALO), 4 * LANES), jnp.bfloat16),
            pltpu.VMEM((refs, 2 * windows * (rows + 2 * HALO), 2 * LANES), jnp.float32),
            pltpu.VMEM((levels, rows, half), jnp.float32),
            pltpu.VMEM((2 * own_levels, rows, half), jnp.float32),
            pltpu.VMEM((own_levels, depths, rows, half), jnp.float32),
            dma((streams,)),
            dma((2, levels)),
            dma((2, 2, own_levels)),
            dma((2 * own_levels,)),
            dma((levels // 2, 2)),
            dma((levels // 2, 2)),
            dma((streams, 2)),
            dma((2, streams, 2)),
            dma((own_levels, depths)),
            dma((levels,)),
            dma((2 * own_levels,)),
        ],
        compiler_params=pltpu.CompilerParams(
            collective_id=0, has_side_effects=True, vmem_limit_bytes=60 * 2**20
        ),
    )(source, receiver, zone, blend, velocities, frequencies)


def local(lat_size, source_field, receiver_field, zone_index, blend_weight, ref_velocity, frequencies):
    return migrate(
        lat_size, lax.axis_size("depth"), source_field, receiver_field, zone_index,
        blend_weight, ref_velocity, frequencies,
    )


def solution(mesh):
    in_specs = (
        P(None, None, "lat", None),
        P(None, None, "lat", None),
        P("depth", "lat", None),
        P("depth", "lat", None),
        P(),
        P(),
    )
    out_specs = P("depth", "lat", None)
    return jax.shard_map(
        functools.partial(local, mesh.shape["lat"]),
        mesh=mesh, in_specs=in_specs, out_specs=out_specs, check_vma=False,
    )
```

```python
import functools
import math

import jax
import jax.numpy as jnp
from jax import lax
from jax.experimental import pallas as pl
from jax.experimental.pallas import tpu as pltpu
from jax.sharding import PartitionSpec as P

HALF = 7
BLEND = 16
LANES = 128
PAD = 128
STEP = LANES - 2 * HALF
HALO = 8
GROUP = 16
FAR = 16
AHEAD = 2

cell_width = 5.0
depth_step = 10.0
taper_width = 16.0


def two_parts(x):
    high = x.astype(jnp.bfloat16)
    return high, (x - high.astype(jnp.float32)).astype(jnp.bfloat16)


def taps_of(frequency, velocity):
    shape = (8, LANES)
    lane = lax.broadcasted_iota(jnp.int32, shape, 1)
    wavenumber = jnp.full(shape, 2.0 * math.pi * frequency) / jnp.full(shape, velocity)
    curvature = wavenumber * (cell_width * cell_width / (2.0 * depth_step))
    phase_turn = wavenumber * depth_step
    offset = jnp.minimum(lane, HALF + 1).astype(jnp.float32)
    envelope = jnp.where(lane <= HALF, jnp.exp(-offset * offset / taper_width), 0.0)
    angle = curvature * (offset * offset)
    raw_re = envelope * jnp.cos(angle)
    raw_im = envelope * jnp.sin(angle)
    sides = jnp.where(lane == 0, 1.0, 2.0)
    sum_re = jnp.sum(sides * raw_re, axis=1, keepdims=True)
    sum_im = jnp.sum(sides * raw_im, axis=1, keepdims=True)
    magnitude = jnp.sqrt(sum_re * sum_re + sum_im * sum_im)
    c_re, c_im = raw_re / magnitude, raw_im / magnitude
    turn_cos, turn_sin = jnp.cos(phase_turn), jnp.sin(phase_turn)
    return c_re, c_im, c_re * turn_cos - c_im * turn_sin, c_re * turn_sin + c_im * turn_cos


def banded(taps, distance):
    out = jnp.zeros(distance.shape, jnp.float32)
    for m in range(HALF + 1):
        tap = jnp.broadcast_to(taps[0:1, m : m + 1], distance.shape)
        out = jnp.where(distance == m, tap, out)
    return out


def set_matrices(at, frequency, velocity, x_mat, y_mat):
    c_re, c_im, d_re, d_im = taps_of(frequency, velocity)
    shape = (GROUP, 12 * GROUP)
    lane = lax.broadcasted_iota(jnp.int32, shape, 1)
    row = lax.broadcasted_iota(jnp.int32, shape, 0)
    distance = jnp.abs(lax.rem(lane, 2 * GROUP) - HALO - row)
    a_re, a_im = banded(c_re, distance), banded(c_im, distance)
    from_re = lax.rem(lane, 4 * GROUP) < 2 * GROUP
    for c, value in enumerate(
        (jnp.where(from_re, a_re, -a_im), jnp.where(from_re, a_im, a_re))
    ):
        high = value.astype(jnp.bfloat16).astype(jnp.float32)
        x_mat[at, c * GROUP : (c + 1) * GROUP] = jnp.where(
            lane < 8 * GROUP, high, value - high
        ).astype(jnp.bfloat16)
    shape = (LANES, LANES)
    k = lax.broadcasted_iota(jnp.int32, shape, 0)
    n = lax.broadcasted_iota(jnp.int32, shape, 1)
    distance = jnp.where(n < STEP, jnp.abs(k - HALF - n), 2 * LANES)
    b_re, b_im = banded(d_re, distance), banded(d_im, distance)
    for c, pair in enumerate(((b_re, b_im), (-b_im, b_re))):
        for o, value in enumerate(pair):
            for p, part in enumerate((0, 0, 1)):
                y_mat[
                    at,
                    (2 * p + c) * LANES : (2 * p + c + 1) * LANES,
                    o * LANES : (o + 1) * LANES,
                ] = two_parts(value)[part]


def body(
    lat_size, refs, source, receiver, zone, blend, velocities, frequencies,
    image, x_mat, y_mat, field, middle, halo, table, rim, weights, xbuf, ybuf, part, inbox, arrived,
    load_sem, table_sem, table_sent, passed_sent, rim_sem, rim_sent,
    send_sem, recv_sem, part_sem, part_sent, inbox_sem,
):
    own_levels, rows, cols = zone.shape
    levels, width_all = table.shape[1], table.shape[3]
    depths = levels // own_levels
    pairs = y_mat.shape[0] // refs
    half = part.shape[2]
    windows = -(-width_all // STEP)
    lat = lax.axis_index("lat")
    me = lax.axis_index("depth")
    side, core = me // 2, lax.rem(me, 2)
    has_up = lat > 0
    has_down = lat < lat_size - 1
    inner = pl.ds(PAD, width_all)

    def columns_of(device):
        return pl.ds(pl.multiple_of((device // 2) * (cols - width_all), LANES), width_all)

    peers = [side * 2 + 1 - core, (1 - side) * 2 + core, (1 - side) * 2 + 1 - core]
    tables = (zone, blend)

    loads = [
        pltpu.make_async_copy(
            ref.at[:, core * pairs + q, :, columns_of(me)],
            field.at[2 * q + f, :, :, inner],
            load_sem.at[2 * q + f],
        )
        for q in range(pairs)
        for f, ref in enumerate((source, receiver))
    ]
    for load in loads:
        load.start()

    def own_table(a, n):
        at = me * own_levels + n
        return pltpu.make_async_copy(
            tables[a].at[n, :, columns_of(me)], table.at[a, at], table_sem.at[a, at]
        )

    partner = peers[0]
    far_levels = 2 * own_levels

    def peer_table(across, a, n):
        at = me * own_levels + n
        peer = (1 - side) * 2 + a if across else partner
        return pltpu.make_async_remote_copy(
            src_ref=tables[a].at[n, :, columns_of(peer)],
            dst_ref=table.at[a, at],
            send_sem=table_sent.at[int(across), a, n],
            recv_sem=table_sem.at[a, at],
            device_id={"depth": peer},
        )

    def passed(i):
        at = (1 - side) * far_levels + i
        return pltpu.make_async_remote_copy(
            src_ref=table.at[core, at],
            dst_ref=table.at[core, at],
            send_sem=passed_sent.at[i],
            recv_sem=table_sem.at[core, at],
            device_id={"depth": partner},
        )

    def pass_on(i):
        at = (1 - side) * far_levels + i
        there = table.at[core, at]
        pltpu.make_async_copy(there, there, table_sem.at[core, at]).wait()
        passed(i).start()

    for n in range(own_levels):
        for a in range(2):
            own_table(a, n).start()
    halo[...] = jnp.zeros_like(halo)
    rim[...] = jnp.full(rim.shape, -2, jnp.int32)
    for ref in (field, middle):
        outside = jnp.zeros((ref.shape[2], PAD), jnp.float32)
        for s in range(2 * pairs):
            for c in range(2):
                ref[s, c, :, 0:PAD] = outside
                ref[s, c, :, PAD + width_all :] = outside

    barrier = pltpu.get_barrier_semaphore()

    @pl.when(has_up)
    def _():
        pl.semaphore_signal(barrier, inc=1, device_id={"lat": lat - 1})

    @pl.when(has_down)
    def _():
        pl.semaphore_signal(barrier, inc=1, device_id={"lat": lat + 1})

    for peer in peers:
        pl.semaphore_signal(barrier, inc=1, device_id={"depth": peer})
    pl.semaphore_wait(
        barrier, len(peers) + has_up.astype(jnp.int32) + has_down.astype(jnp.int32)
    )

    def to_up(s, slot, count):
        return pltpu.make_async_remote_copy(
            src_ref=field.at[s, :, pl.ds(0, count), inner],
            dst_ref=halo.at[slot, s, 1, :, pl.ds(0, count), inner],
            send_sem=send_sem.at[s, 0],
            recv_sem=recv_sem.at[slot, s, 1],
            device_id={"lat": lat - 1},
        )

    def to_down(s, slot, count):
        return pltpu.make_async_remote_copy(
            src_ref=field.at[s, :, pl.ds(rows - count, count), inner],
            dst_ref=halo.at[slot, s, 0, :, pl.ds(FAR - count, count), inner],
            send_sem=send_sem.at[s, 1],
            recv_sem=recv_sem.at[slot, s, 0],
            device_id={"lat": lat + 1},
        )

    def each_side(act_up, act_down):
        @pl.when(has_up)
        def _():
            act_up()

        @pl.when(has_down)
        def _():
            act_down()

    def send(s, slot, count):
        each_side(
            lambda: to_up(s, slot, count).start(), lambda: to_down(s, slot, count).start()
        )

    def wait_sent(s, slot, count):
        each_side(
            lambda: to_up(s, slot, count).wait_send(),
            lambda: to_down(s, slot, count).wait_send(),
        )

    def wait_arrived(s, slot, count):
        each_side(
            lambda: to_down(s, slot, count).wait_recv(),
            lambda: to_up(s, slot, count).wait_recv(),
        )

    def rim_up(h):
        return pltpu.make_async_remote_copy(
            src_ref=table.at[:, 2 * h, pl.ds(0, HALO)],
            dst_ref=rim.at[h, 1],
            send_sem=rim_sent.at[h, 0],
            recv_sem=rim_sem.at[h, 1],
            device_id={"lat": lat - 1},
        )

    def rim_down(h):
        return pltpu.make_async_remote_copy(
            src_ref=table.at[:, 2 * h, pl.ds(rows - HALO, HALO)],
            dst_ref=rim.at[h, 0],
            send_sem=rim_sent.at[h, 1],
            recv_sem=rim_sem.at[h, 0],
            device_id={"lat": lat + 1},
        )

    def need(z):
        for a in range(2):
            taken = jnp.logical_and(z // far_levels != side, core == a)

            @pl.when(jnp.logical_not(taken))
            def _():
                pltpu.make_async_copy(table.at[a, z], table.at[a, z], table_sem.at[a, z]).wait()

    for s in range(2 * pairs):
        loads[s].wait()
        if s % 2 == 1:
            field[s, 1] = -field[s, 1]
        send(s, 0, HALO)
    for n in range(own_levels):
        @pl.when(core == 0)
        def _():
            for a in range(2):
                peer_table(True, a, n).start()

        for a in range(2):
            peer_table(False, a, n).start()

    def prepare(at, carry):
        set_matrices(
            at,
            frequencies[core * pairs + at // refs].astype(jnp.float32),
            velocities[lax.rem(at, refs)],
            x_mat,
            y_mat,
        )
        return carry

    lax.fori_loop(0, pairs * refs, prepare, 0)
    for i in range(AHEAD):
        pass_on(i)

    def part_copy(z):
        return pltpu.make_async_remote_copy(
            src_ref=part.at[z],
            dst_ref=arrived.at[lax.rem(z, own_levels), me],
            send_sem=part_sent.at[z],
            recv_sem=part_sem.at[lax.rem(z, own_levels), me],
            device_id={"depth": z // own_levels},
        )

    def set_weights(z, pieces):
        count = rows + (2 * HALO if pieces else 0)
        for w in range(windows):
            width = min(STEP, width_all - w * STEP)
            here = pl.ds(w * STEP, width)
            both = []
            for a in range(2):
                value = table[a, z, :, here]
                if pieces:
                    value = jnp.concatenate(
                        [rim[z // 2, 0, a, :, here], value, rim[z // 2, 1, a, :, here]], 0
                    )
                both.append(value)
            which = both[0]
            upper = both[1].astype(jnp.float32) * (1.0 / BLEND)
            lower = 1.0 - upper
            for j in range(refs):
                weights[int(pieces), j, w * count : (w + 1) * count, 0:width] = jnp.where(
                    which == j, lower, jnp.where(which == j - 1, upper, 0.0)
                )

    def advance(q, wide_step, read, before_write, target, streams):
        groups = 3 if wide_step else 2
        count = groups * GROUP
        used = windows * count
        split = {}
        units = [(i, w, g) for i in range(len(streams)) for w in range(windows) for g in range(groups)]
        for first in range(0, len(units), 2):
            chosen = units[first : first + 2]
            highs, lows = [], []
            for i, w, g in chosen:
                if (i, w) not in split:
                    at = pl.ds(PAD + w * STEP - HALF, LANES)
                    split[i, w] = [two_parts(read(streams[i], c, at)) for c in range(2)]
                taken = slice(g * GROUP, (g + 2) * GROUP)
                highs.append(jnp.concatenate([both[0][taken] for both in split[i, w]], 0))
                lows.append(jnp.concatenate([both[1][taken] for both in split[i, w]], 0))
            high, low = jnp.concatenate(highs, 1), jnp.concatenate(lows, 1)
            out = jnp.dot(
                x_mat[q * refs : (q + 1) * refs].reshape(2 * refs * GROUP, 12 * GROUP),
                jnp.concatenate([high, low, high], 0),
                preferred_element_type=jnp.float32,
            )
            for p, values in enumerate(two_parts(out)):
                for j in range(refs):
                    for c in range(2):
                        for n, (i, w, g) in enumerate(chosen):
                            top = (j * 2 + c) * GROUP
                            row = i * used + w * count + g * GROUP
                            xbuf[
                                j,
                                row : row + GROUP,
                                (p * 2 + c) * LANES : (p * 2 + c + 1) * LANES,
                            ] = values[top : top + GROUP, n * LANES : (n + 1) * LANES]
        before_write()
        every = len(streams) * used
        for j in range(refs):
            ybuf[j, 0:every] = jnp.dot(
                jnp.concatenate([xbuf[j, 0:every], xbuf[j, 0:every, 0 : 2 * LANES]], 1),
                y_mat[q * refs + j],
                preferred_element_type=jnp.float32,
            )
        for i, s in enumerate(streams):
            for w in range(windows):
                width = min(STEP, width_all - w * STEP)
                block = slice(w * count, (w + 1) * count)
                made = slice(i * used + w * count, i * used + (w + 1) * count)
                for c in range(2):
                    total = None
                    for j in range(refs):
                        term = (
                            weights[int(wide_step), j, block, 0:width]
                            * ybuf[j, made, c * LANES : c * LANES + width]
                        )
                        total = term if total is None else total + term
                    target[s, c, :, pl.ds(PAD + w * STEP, width)] = total

    def to_partner(z):
        return pltpu.make_async_remote_copy(
            src_ref=part.at[z],
            dst_ref=inbox.at[lax.rem(z, far_levels)],
            send_sem=part_sent.at[z],
            recv_sem=inbox_sem.at[lax.rem(z, far_levels)],
            device_id={"depth": partner},
        )

    def image_of(z, ref, from_row):
        mine = pl.ds(pl.multiple_of(PAD + side * (width_all - half), LANES), half)
        taken = pl.ds(from_row, rows)
        total = jnp.zeros((rows, half), jnp.float32)
        for q in range(pairs):
            total = total + ref[2 * q, 0, taken, mine] * ref[2 * q + 1, 0, taken, mine]
            total = total - ref[2 * q, 1, taken, mine] * ref[2 * q + 1, 1, taken, mine]

        @pl.when(z // own_levels == me)
        def _():
            arrived[lax.rem(z, own_levels), me] = total

        @pl.when(z // own_levels != me)
        def _():
            part[z] = total

        @pl.when(jnp.logical_and(z // far_levels == side, z // own_levels != me))
        def _():
            part_copy(z).start()

        @pl.when(jnp.logical_and(z // far_levels != side, lax.rem(z, 2) != core))
        def _():
            to_partner(z).start()

    def finish(z):
        @pl.when(jnp.logical_and(z // far_levels != side, lax.rem(z, 2) == core))
        def _():
            to_partner(z).wait_recv()
            part[z] = part[z] + inbox[lax.rem(z, far_levels)]
            part_copy(z).start()

    single = 2

    def one_level(z, carry):
        slot = lax.rem(z, 2)

        @pl.when(jnp.logical_and(core == 1, 2 * z < own_levels))
        def _():
            for n in range(2):
                for a in range(2):
                    peer_table(True, a, 2 * z + n).start()

        @pl.when(z + AHEAD < far_levels)
        def _():
            pass_on(z + AHEAD)

        need(z)
        set_weights(z, False)

        @pl.when(z == single - 1)
        def _():
            need(single)
            each_side(
                lambda: rim_up(single // 2).start(), lambda: rim_down(single // 2).start()
            )

        for s in range(2 * pairs):
            wait_arrived(s, slot, HALO)

            def read_field(s, c, at):
                return jnp.concatenate(
                    [
                        halo[slot, s, 0, c, FAR - HALO :, at],
                        field[s, c, :, at],
                        halo[slot, s, 1, c, 0:HALO, at],
                    ],
                    0,
                )

            advance(s // 2, False, read_field, lambda: wait_sent(s, slot, HALO), field, [s])

            @pl.when(z < single - 1)
            def _():
                send(s, 1 - slot, HALO)

            @pl.when(z == single - 1)
            def _():
                send(s, 1 - slot, FAR)

        image_of(z, field, 0)

        @pl.when(z > 0)
        def _():
            finish(z - 1)

        return carry

    lax.fori_loop(0, single, one_level, 0)

    def two_levels(h, carry):
        slot = lax.rem(h - single // 2, 2)
        z = 2 * h
        each_side(lambda: rim_down(h).wait_recv(), lambda: rim_up(h).wait_recv())
        set_weights(z, True)

        def read_wide(s, c, at):
            return jnp.concatenate(
                [halo[slot, s, 0, c, :, at], field[s, c, :, at], halo[slot, s, 1, c, :, at]], 0
            )

        def read_middle(s, c, at):
            return middle[s, c, :, at]

        for streams in ([0], [1], [2], [3]):
            q = streams[0] // 2

            def all_sent():
                for s in streams:
                    wait_sent(s, slot, FAR)

            for s in streams:
                wait_arrived(s, slot, FAR)
            advance(q, True, read_wide, lambda: None, middle, streams)
            if streams[0] == 0:
                need(z + 1)
                set_weights(z + 1, False)
                for ahead in range(AHEAD, 2 * AHEAD):
                    @pl.when(z + ahead < far_levels)
                    def _():
                        pass_on(z + ahead)

            if streams[-1] == 1:
                @pl.when(z + 2 < levels)
                def _():
                    need(z + 2)
                    each_side(lambda: rim_up(h + 1).start(), lambda: rim_down(h + 1).start())

            advance(q, False, read_middle, all_sent, field, streams)

            @pl.when(z + 2 < levels)
            def _():
                for s in streams:
                    send(s, 1 - slot, FAR)

        image_of(z, middle, HALO)
        image_of(z + 1, field, 0)
        finish(z - 1)

        @pl.when(z > single)
        def _():
            finish(z - 2)

        return carry

    lax.fori_loop(single // 2, levels // 2, two_levels, 0)

    finish(levels - 2)
    finish(levels - 1)
    for h in range(single // 2, levels // 2):
        each_side(lambda: rim_up(h).wait_send(), lambda: rim_down(h).wait_send())
    for n in range(own_levels):
        for a in range(2):
            peer_table(False, a, n).wait_send()
            peer_table(True, a, n).wait_send()
    for i in range(far_levels):
        passed(i).wait_send()

    def sent(z, carry):
        @pl.when(z // own_levels != me)
        def _():
            part_copy(z).wait_send()

        return carry

    lax.fori_loop(0, levels, sent, 0)
    for n in range(own_levels):
        for d in range(depths):
            comes = jnp.logical_or(side == d // 2, d % 2 == n % 2)

            @pl.when(jnp.logical_and(d != me, comes))
            def _():
                pltpu.make_async_copy(
                    arrived.at[n, d], arrived.at[n, d], part_sem.at[n, d]
                ).wait()

        for h in range(depths // 2):
            there = slice(h * half, (h + 1) * half)

            @pl.when(side == h)
            def _():
                image[n, :, there] = (arrived[n, 2 * h] + arrived[n, 2 * h + 1]) * (
                    1.0 / (2 * pairs)
                )

            @pl.when(side != h)
            def _():
                image[n, :, there] = arrived[n, 2 * h + n % 2] * (1.0 / (2 * pairs))


def migrate(lat_size, depths, source, receiver, zone, blend, velocities, frequencies):
    own_levels, rows, cols = zone.shape
    levels = depths * own_levels
    refs = velocities.shape[0]
    pairs = frequencies.shape[0] // 2
    streams = 2 * pairs
    half = cols // 2
    width = half + -(-HALF * levels // LANES) * LANES
    windows = -(-width // STEP)
    vmem = pl.BlockSpec(memory_space=pltpu.VMEM)
    smem = pl.BlockSpec(memory_space=pltpu.SMEM)
    hbm = pl.BlockSpec(memory_space=pl.ANY)
    wide = width + 2 * PAD
    dma = pltpu.SemaphoreType.DMA
    return pl.pallas_call(
        functools.partial(body, lat_size, refs),
        out_shape=jax.ShapeDtypeStruct((own_levels, rows, cols), jnp.float32),
        in_specs=[hbm, hbm, hbm, hbm, smem, smem],
        out_specs=vmem,
        scratch_shapes=[
            pltpu.VMEM((pairs * refs, 2 * GROUP, 12 * GROUP), jnp.bfloat16),
            pltpu.VMEM((pairs * refs, 6 * LANES, 2 * LANES), jnp.bfloat16),
            pltpu.VMEM((streams, 2, rows, wide), jnp.float32),
            pltpu.VMEM((streams, 2, rows + 2 * HALO, wide), jnp.float32),
            pltpu.VMEM((2, streams, 2, 2, FAR, wide), jnp.float32),
            pltpu.VMEM((2, levels, rows, width), jnp.int32),
            pltpu.VMEM((levels // 2, 2, 2, HALO, width), jnp.int32),
            pltpu.VMEM((2, refs, windows * (rows + 2 * HALO), LANES), jnp.float32),
            pltpu.VMEM((refs, 2 * windows * (rows + 2 * HALO), 4 * LANES), jnp.bfloat16),
            pltpu.VMEM((refs, 2 * windows * (rows + 2 * HALO), 2 * LANES), jnp.float32),
            pltpu.VMEM((levels, rows, half), jnp.float32),
            pltpu.VMEM((2 * own_levels, rows, half), jnp.float32),
            pltpu.VMEM((own_levels, depths, rows, half), jnp.float32),
            dma((streams,)),
            dma((2, levels)),
            dma((2, 2, own_levels)),
            dma((2 * own_levels,)),
            dma((levels // 2, 2)),
            dma((levels // 2, 2)),
            dma((streams, 2)),
            dma((2, streams, 2)),
            dma((own_levels, depths)),
            dma((levels,)),
            dma((2 * own_levels,)),
        ],
        compiler_params=pltpu.CompilerParams(
            collective_id=0, has_side_effects=True, vmem_limit_bytes=60 * 2**20
        ),
    )(source, receiver, zone, blend, velocities, frequencies)


def local(lat_size, source_field, receiver_field, zone_index, blend_weight, ref_velocity, frequencies):
    return migrate(
        lat_size, lax.axis_size("depth"), source_field, receiver_field, zone_index,
        blend_weight, ref_velocity, frequencies,
    )


def solution(mesh):
    in_specs = (
        P(None, None, "lat", None),
        P(None, None, "lat", None),
        P("depth", "lat", None),
        P("depth", "lat", None),
        P(),
        P(),
    )
    out_specs = P("depth", "lat", None)
    return jax.shard_map(
        functools.partial(local, mesh.shape["lat"]),
        mesh=mesh, in_specs=in_specs, out_specs=out_specs, check_vma=False,
    )
```
